32 devices in a mesh: ctx: 8 (over z, x), head: 4 (over y, core).
Axes of the slice: x: 2, y: 2, z: 4, core: 2. Of those that a mesh axis runs over, the one named last changes fastest.
Arguments:
- tokens: bfloat16 [4096, 4096], P('ctx', 'head'), may hold values from -6 to 6
- pair_weight: bfloat16 [4096, 256], replicated, may hold values from -0.09375 to 0.09375
- value_weight: bfloat16 [4096, 4096], P(None, 'head'), may hold values from -0.09375 to 0.09375
- output_weight: bfloat16 [4096, 4096], P('head'), may hold values from -0.09375 to 0.09375
- level_index: int32 [4096, 6], P('ctx'), may hold values from 0 to 15
- level_table: float32 [6, 16, 32], P(None, None, 'head'), may hold values from 0.05 to 1
- out_gain: float32 [4096], P('head'), may hold values from 0.5 to 1.5
Outputs:
- layer_out: bfloat16 [4096, 4096], P('ctx', 'head')
The draws below stay inside these ranges and needn't reach their ends.
All inputs are finite; a program needn't handle non-finite values.
Results may differ from the reference program's by a relative error of at most 0.02.
Values may be sent and summed in bfloat16 or wider, within the bound.
No kernel may reach another device: no remote copies, remote signals or barrier semaphores. Data moves between devices by JAX's collectives and lax.ppermute only.
A program may use at most 128 MiB of HBM per device.

```python
import math
import jax
import jax.numpy as jnp
from jax import lax

D = 4096
HEADS = 32
DH = 128
DK = 128
SPAN = 128
NTAB = 16
TOKENS = 4096
HV = 4096
LOCAL_BITS = 2
CTX_BITS = 3
LEVELS = 6
N_HEAD = 4


def place_ends(values, stream_key, low, largest):
    longest = values.shape.index(max(values.shape))
    spots = []
    for shift in (0, 1):
        where = [jax.random.randint(jax.random.fold_in(stream_key, axis), (), 0, length) for axis, length in enumerate(values.shape)]
        where[longest] = (where[longest] + shift) % values.shape[longest]
        spots.append(tuple(where))
    return values.at[spots[0]].set(low).at[spots[1]].set(largest)


def block_scale(rng, extent, split, smallest, top_value):
    level, own = 1.0, jax.random.fold_in(rng, 6)
    for position, blocks in split:
        draws = jnp.exp(jax.random.uniform(jax.random.fold_in(own, position), (blocks,), jnp.float32, smallest / len(split), top_value / len(split)))
        level = level * jnp.repeat(draws, extent[position] // blocks).reshape([-1 if axis == position else 1 for axis in range(len(extent))])
    return level


def normal_values(stream_key, shape, scale, most, split=(), held_as=jnp.bfloat16):
    factor_of = block_scale(stream_key, shape, split, -0.22, 0.18) if split else 1.0
    drawn = jax.random.normal(stream_key, shape, jnp.float32) * scale * factor_of
    return jnp.minimum(jnp.maximum(drawn, -most), most).astype(held_as)


def setup_inputs(seed: int = 0) -> dict:
    streams_of = jax.random.split(jax.random.key(seed), 8)
    tokens = normal_values(streams_of[0], (TOKENS, D), 1.0, 6.0, ((0, 8), (1, 4)))
    pair_weight = normal_values(streams_of[1], (D, 2 * DK), D ** -0.5, 0.09375)
    value_weight = normal_values(streams_of[2], (D, HV), D ** -0.5, 0.09375, ((1, 4),))
    output_weight = normal_values(streams_of[3], (HV, D), HV ** -0.5, 0.09375, ((0, 4),))
    level_index = place_ends(jax.random.randint(streams_of[4], (TOKENS, LEVELS), 0, NTAB), jax.random.fold_in(streams_of[4], 1), 0, NTAB - 1).astype(jnp.int32)
    level_table = jnp.clip(jnp.exp(math.log(1.0) - 2.9957323 * jax.random.uniform(streams_of[5], (LEVELS, NTAB, HEADS), jnp.float32) ** block_scale(streams_of[5], (LEVELS, NTAB, HEADS), ((2, 4),), -0.2, 0.2)), 0.05, 1.0)
    out_gain = jnp.clip(1.0 + 0.1 * jax.random.normal(streams_of[6], (HV,), jnp.float32), 0.5, 1.5)
    return dict(tokens=tokens, pair_weight=pair_weight, value_weight=value_weight, output_weight=output_weight, level_index=level_index, level_table=level_table, out_gain=out_gain)


EPS = 1e-06

def rounded(values):
    return lax.optimization_barrier(values.astype(jnp.bfloat16)).astype(jnp.float32)

def unit_rows(values):
    scale = lax.rsqrt(lax.optimization_barrier(jnp.mean(values * values, axis=-1, keepdims=True)) + EPS)
    return values * scale / math.sqrt(values.shape[-1])

def reference(tokens, pair_weight, value_weight, output_weight, level_index, level_table, out_gain):
    token_count = TOKENS
    spans = token_count // SPAN
    paired = jnp.dot(tokens, pair_weight, preferred_element_type=jnp.float32)
    queries = rounded(unit_rows(paired[:, :DK]))
    keys_all = rounded(unit_rows(paired[:, DK:]))
    values = rounded(jnp.dot(tokens, value_weight, preferred_element_type=jnp.float32))
    level_ids = jnp.arange(LEVELS, dtype=jnp.int32)
    mixing = level_table[level_ids[None, :], level_index]
    query_blocks = queries.reshape(spans, SPAN, DK)
    key_blocks = keys_all.reshape(spans, SPAN, DK)
    scores = jnp.einsum('ncd,ned->nce', query_blocks, key_blocks)
    causal = jnp.arange(SPAN)[:, None] >= jnp.arange(SPAN)[None, :]
    scores = rounded(jnp.where(causal[None], scores, 0.0))
    span_ids = jnp.arange(spans, dtype=jnp.int32)
    head_values = values.reshape(token_count, HEADS, DH).transpose(1, 0, 2)
    head_mixing = mixing.transpose(2, 0, 1)

    def one_head(inputs):
        value_rows, weight_rows = inputs
        value_blocks = value_rows.reshape(spans, SPAN, DH)
        result = jnp.einsum('nce,nev->ncv', scores, value_blocks).reshape(token_count, DH)
        result = result * weight_rows[:, 0:1]
        states = jnp.einsum('ncd,ncv->ndv', key_blocks, value_blocks)
        for level_bit in range(LOCAL_BITS + CTX_BITS):
            block_width = 2 ** level_bit
            sums = states.reshape(spans // block_width, block_width, DK, DH).sum(axis=1)
            shifted = span_ids // block_width
            present = (shifted % 2).astype(jnp.float32)
            bucket = sums[jnp.maximum(shifted - 1, 0)] * present[:, None, None]
            bucket = rounded(bucket)
            readout = jnp.einsum('ncd,ndv->ncv', query_blocks, bucket).reshape(token_count, DH)
            result = result + weight_rows[:, level_bit + 1:level_bit + 2] * readout
        return result
    mixed = lax.map(one_head, (head_values, head_mixing)).transpose(1, 0, 2)
    normed = mixed * lax.rsqrt(lax.optimization_barrier(jnp.mean(mixed * mixed, axis=-1, keepdims=True)) + EPS)
    normed = normed * out_gain.reshape(HEADS, DH)
    hidden = normed.reshape(token_count, HEADS * DH).astype(jnp.bfloat16)
    group_width = HEADS * DH // N_HEAD
    accumulated = jnp.zeros((token_count, D), jnp.float32)
    for group_index in range(N_HEAD):
        lower_end = group_index * group_width
        partial_value = jnp.dot(hidden[:, lower_end:lower_end + group_width], output_weight[lower_end:lower_end + group_width], preferred_element_type=jnp.float32)
        accumulated = accumulated + rounded(partial_value)
    return accumulated.astype(jnp.bfloat16)
```

```python
import functools
import math

import jax
import jax.numpy as jnp
from jax import lax
from jax.experimental import pallas as pl
from jax.experimental.pallas import tpu as pltpu
from jax.sharding import PartitionSpec as P

DH = 128
DK = 128
SPAN = 128
EPS = 1e-06
MIB = 1 << 20


F32 = jnp.float32
BF16 = jnp.bfloat16


def swap(value, axis, mask, upward=False):
    pairs = [(s, s ^ mask) for s in range(lax.axis_size(axis)) if not (upward and s & mask)]
    return lax.ppermute(value, axis, pairs)


def after(value, *earlier):
    return lax.optimization_barrier((value, *earlier))[0]


def unit_rows(values):
    scale = lax.rsqrt(jnp.mean(values * values, axis=-1, keepdims=True) + EPS)
    return values * scale / math.sqrt(values.shape[-1])


def mm(a, b):
    return jnp.dot(a, b, preferred_element_type=F32)


def mm_t(a, b):
    return lax.dot_general(a, b, (((0,), (0,)), ((), ())), preferred_element_type=F32)


def params(limit):
    return pltpu.CompilerParams(vmem_limit_bytes=limit * MIB)


def cost(flops, nbytes):
    return pl.CostEstimate(flops=flops, bytes_accessed=nbytes, transcendentals=0)


def full(shape):
    return pl.BlockSpec(shape, lambda *_: (0,) * len(shape))


def key_part_kernel(head_ref, x_ref, w_ref, out_ref):
    out_ref[...] = mm(x_ref[...], w_ref[...]).astype(BF16)


def key_part(head, tokens, pair_weight):
    rows, feat = tokens.shape
    return pl.pallas_call(
        key_part_kernel,
        out_shape=jax.ShapeDtypeStruct((rows, DK), BF16),
        grid_spec=pltpu.PrefetchScalarGridSpec(
            num_scalar_prefetch=1,
            grid=(1,),
            in_specs=[full((rows, feat)), pl.BlockSpec((feat, DK), lambda i, h: (h[0], 1))],
            out_specs=full((rows, DK)),
        ),
        compiler_params=params(12),
        cost_estimate=cost(2 * rows * feat * DK, 2 * rows * feat),
        name="key_part",
    )(head, tokens, pair_weight)


def key_tokens_kernel(*refs):
    *part_refs, x_ref, out_ref = refs
    total = part_refs[0][...].astype(F32)
    for ref in part_refs[1:]:
        total = total + ref[...].astype(F32)
    keys = unit_rows(total).astype(BF16)
    out_ref[...] = mm_t(keys, x_ref[...]).astype(BF16)


def key_tokens(parts, tokens):
    rows, feat = tokens.shape
    return pl.pallas_call(
        key_tokens_kernel,
        out_shape=jax.ShapeDtypeStruct((DK, feat), BF16),
        compiler_params=params(12),
        cost_estimate=cost(2 * rows * feat * DK, 2 * rows * feat),
        name="key_tokens",
    )(*parts, tokens)


def block_dot_kernel(n, has_acc, offsets, head_ref, *refs):
    lhs = refs[:n]
    w_ref = refs[n]
    acc_ref = refs[n + 1] if has_acc else None
    out_ref = refs[-1]
    step = pl.program_id(0)
    for e in range(n):

        @pl.when(step == e)
        def _(e=e):
            part = mm(lhs[e][...], w_ref[...])
            if e == 0:
                out_ref[...] = part + acc_ref[...] if has_acc else part
            else:
                out_ref[...] += part


def block_dot(head, lhs, weight, offsets, acc=None, limit=24, name=None):
    rows, feat = lhs[0].shape
    width = weight.shape[1]
    n = len(lhs)
    first = offsets[0]
    operands = [head, *lhs, weight]
    specs = [full((rows, feat))] * n + [
        pl.BlockSpec((feat, width), lambda i, h: (h[0] ^ (i + first), 0))
    ]
    if acc is not None:
        operands.append(acc)
        specs.append(full((rows, width)))
    return pl.pallas_call(
        functools.partial(block_dot_kernel, n, acc is not None, offsets),
        out_shape=jax.ShapeDtypeStruct((rows, width), F32),
        grid_spec=pltpu.PrefetchScalarGridSpec(
            num_scalar_prefetch=1, grid=(n,), in_specs=specs, out_specs=full((rows, width))
        ),
        compiler_params=params(limit),
        cost_estimate=cost(2 * rows * feat * width * n, 2 * n * feat * width),
        name=name,
    )(*operands)


def span_kernel(n, chunks, head_ref, *refs):
    x0, x1 = refs[0], refs[1]
    far = refs[2 : 2 + (n - 2) * chunks]
    rest = refs[2 + (n - 2) * chunks :]
    w_ref, p_ref, acc_ref, mix_ref, q_ref, out_ref, xs, vacc, pacc = rest
    step = pl.program_id(0)
    rows = xs.shape[0]
    width = vacc.shape[1]

    @pl.when(step == 0)
    def _():
        pacc[...] = mm(x0[...], p_ref[...])

    @pl.when(step == 1)
    def _():
        pacc[...] += mm(x1[...], p_ref[...])
        vacc[...] = acc_ref[...]

    for e in range(2, n):

        @pl.when(step == e)
        def _(e=e):
            for c in range(chunks):
                size = rows // chunks
                xs[c * size : (c + 1) * size] = far[(e - 2) * chunks + c][...]
            pacc[...] += mm(xs[...], p_ref[...])
            vacc[...] += mm(xs[...], w_ref[...])

    @pl.when(step == n - 1)
    def _():
        spans = rows // SPAN
        bits = spans.bit_length() - 1
        heads = width // DH
        queries = unit_rows(pacc[:, :DK]).astype(BF16)
        keys = unit_rows(pacc[:, DK:]).astype(BF16)
        q_ref[...] = queries
        causal = (
            lax.broadcasted_iota(jnp.int32, (SPAN, SPAN), 0)
            >= lax.broadcasted_iota(jnp.int32, (SPAN, SPAN), 1)
        )
        states = []
        for c in range(spans):
            at = slice(c * SPAN, (c + 1) * SPAN)
            vals = vacc[at].astype(BF16)
            scores = lax.dot_general(
                queries[at], keys[at], (((1,), (1,)), ((), ())), preferred_element_type=F32
            )
            scores = jnp.where(causal, scores, 0.0).astype(BF16)
            reads = [(0, mm(scores, vals))]
            for b in range(bits):
                if c >> b & 1:
                    top = c >> b << b
                    bucket = states[top - (1 << b)]
                    for j in range(top - (1 << b) + 1, top):
                        bucket = bucket + states[j]
                    reads.append((1 + b, mm(queries[at], bucket.astype(BF16))))
            if c < spans - 1:
                states.append(mm_t(keys[at], vals))
            for h in range(heads):
                cols = slice(h * DH, (h + 1) * DH)
                total = None
                for level, value in reads:
                    col = level * heads + h
                    part = value[:, cols] * mix_ref[at, col : col + 1]
                    total = part if total is None else total + part
                out_ref[at, cols] = total


def span_part(head, near, far, value_weight, pair_weight, acc, mixing):
    rows, feat = near[0].shape
    width = value_weight.shape[1]
    n = value_weight.shape[0] // feat
    chunks = len(far) // (n - 2)
    specs = (
        [full((rows, feat))] * 2
        + [full((rows // chunks, feat))] * len(far)
        + [
            pl.BlockSpec((feat, width), lambda i, h: (h[0] ^ jnp.maximum(i, 2), 0)),
            pl.BlockSpec((feat, 2 * DK), lambda i, h: (h[0] ^ i, 0)),
            full((rows, width)),
            full(mixing.shape),
        ]
    )
    return pl.pallas_call(
        functools.partial(span_kernel, n, chunks),
        out_shape=(
            jax.ShapeDtypeStruct((rows, DK), BF16),
            jax.ShapeDtypeStruct((rows, width), F32),
        ),
        grid_spec=pltpu.PrefetchScalarGridSpec(
            num_scalar_prefetch=1,
            grid=(n,),
            in_specs=specs,
            out_specs=(full((rows, DK)), full((rows, width))),
            scratch_shapes=[
                pltpu.VMEM((rows, feat), BF16),
                pltpu.VMEM((rows, width), F32),
                pltpu.VMEM((rows, 2 * DK), F32),
            ],
        ),
        compiler_params=params(40),
        cost_estimate=cost(2 * rows * feat * width * (n - 2), 2 * (n - 2) * feat * width),
        name="span_part",
    )(head, *near, *far, value_weight, pair_weight, acc, mixing)


def hidden_kernel(n_far, pieces, first_level, q_ref, *refs):
    far = refs[: n_far * pieces]
    mix_ref, near_ref, gain_ref, out_ref = refs[n_far * pieces :]
    width = out_ref.shape[1]
    heads = width // DH
    per = heads // pieces
    for h in range(heads):
        cols = slice(h * DH, (h + 1) * DH)
        total = near_ref[:, cols]
        g, k = divmod(h, per)
        for b in range(n_far):
            col = (first_level + b) * heads + h
            value = mm(q_ref[...], far[b * pieces + g][:, k * DH : (k + 1) * DH])
            total = total + value * mix_ref[:, col : col + 1]
        scale = lax.rsqrt(jnp.mean(total * total, axis=-1, keepdims=True) + EPS)
        out_ref[:, cols] = (total * scale * gain_ref[:, cols]).astype(BF16)


def hidden_part(i, chunks, queries, far, pieces, mixing, near, gain, first_level):
    rows, width = near.shape
    size = rows // chunks
    n_far = len(far) // pieces

    def block(cols):
        return pl.BlockSpec((size, cols), lambda k: (i, 0))

    return pl.pallas_call(
        functools.partial(hidden_kernel, n_far, pieces, first_level),
        out_shape=jax.ShapeDtypeStruct((size, width), BF16),
        grid=(1,),
        in_specs=[block(DK)]
        + [full(f.shape) for f in far]
        + [block(mixing.shape[1]), block(width), full((1, width))],
        out_specs=full((size, width)),
        compiler_params=params(12),
        cost_estimate=cost(2 * size * DK * width * n_far, 6 * size * width),
        name="hidden_part",
    )(queries, *far, mixing, near, gain)


def out_kernel(chunks, head_ref, *refs):
    own, other = refs[:chunks], refs[chunks : 2 * chunks]
    w_ref, v_ref, out_ref = refs[2 * chunks : 2 * chunks + 3]
    size = own[0].shape[0]
    if chunks == 1:
        a, b = own[0][...], other[0][...]
    else:
        xa, xb = refs[2 * chunks + 3 :]
        for c in range(chunks):
            xa[c * size : (c + 1) * size] = own[c][...]
            xb[c * size : (c + 1) * size] = other[c][...]
        a, b = xa[...], xb[...]
    out_ref[...] = (mm(a, w_ref[...]) + mm(b, v_ref[...])).astype(out_ref.dtype)


def out_part(head, own, other, weight, weight_other, mask, block, dtype):
    chunks = len(own)
    size, width = own[0].shape
    tiles = 2
    tile = block // tiles
    spec = pl.BlockSpec((width, tile), lambda k, h: (0, (h[0] ^ mask) * tiles + k))
    return pl.pallas_call(
        functools.partial(out_kernel, chunks),
        out_shape=jax.ShapeDtypeStruct((size * chunks, block), dtype),
        grid_spec=pltpu.PrefetchScalarGridSpec(
            num_scalar_prefetch=1,
            grid=(tiles,),
            in_specs=[full((size, width))] * (2 * chunks) + [spec, spec],
            out_specs=pl.BlockSpec((size * chunks, tile), lambda k, h: (0, k)),
            scratch_shapes=[pltpu.VMEM((size * chunks, width), BF16)] * (2 if chunks > 1 else 0),
        ),
        compiler_params=params(20),
        cost_estimate=cost(4 * size * chunks * width * block, 4 * width * block),
        name="out_part",
    )(head, *own, *other, weight, weight_other)


def sum_kernel(chunks, acc_ref, *refs):
    out_ref = refs[-1]
    size = out_ref.shape[0] // chunks
    for c in range(chunks):
        at = slice(c * size, (c + 1) * size)
        total = acc_ref[at]
        for ref in refs[c:-1:chunks]:
            total = total + ref[...].astype(F32)
        out_ref[at] = total.astype(BF16)


def sum_part(acc, arrived, chunks):
    return pl.pallas_call(
        functools.partial(sum_kernel, chunks),
        out_shape=jax.ShapeDtypeStruct(acc.shape, BF16),
        compiler_params=params(12),
        cost_estimate=cost(acc.size, 8 * acc.size),
        name="sum_part",
    )(acc, *arrived)


CHUNKS = 4
PIECES = 2


def local(tokens, pair_weight, value_weight, output_weight, level_index, level_table, out_gain):
    rows, feat = tokens.shape
    width = value_weight.shape[1]
    heads = width // DH
    n_head = lax.axis_size("head")
    ctx_bits = lax.axis_size("ctx").bit_length() - 1
    levels = level_table.shape[0]
    head = lax.axis_index("head").astype(jnp.int32).reshape(1)
    size = rows // CHUNKS
    block = output_weight.shape[1] // n_head

    tokens_c = swap(tokens, "head", 1)
    own_key = key_part(head, tokens, pair_weight)
    parts = [own_key, swap(own_key, "head", 1)]
    for mask in range(2, n_head, 2):
        got = swap(own_key, "head", mask)
        parts += [got, swap(got, "head", 1)]

    far_x = []
    for mask in range(2, n_head, 2):
        got = [swap(tokens[c * size : (c + 1) * size], "head", mask) for c in range(CHUNKS)]
        far_x += got + [swap(g, "head", 1) for g in got]

    table_ids = jnp.arange(level_table.shape[1], dtype=jnp.int32)
    onehot = (level_index[:, :, None] == table_ids[None, None, :]).astype(F32)
    mixing = jnp.einsum("tln,lnh->tlh", onehot, level_table, precision=lax.Precision.HIGHEST)
    mixing = mixing.reshape(rows, levels * heads)

    acc = block_dot(head, [tokens, tokens_c], value_weight, (0, 1), limit=24, name="value_near")

    kx = key_tokens(parts, tokens)
    kx_c = swap(kx, "head", 1)
    kx_far = []
    for mask in range(2, n_head, 2):
        got = swap(kx, "head", mask)
        kx_far += [got, swap(got, "head", 1)]
    total = block_dot(head, [kx, kx_c], value_weight, (0, 1), limit=12, name="total_near")
    total = block_dot(
        head, kx_far, value_weight, tuple(range(2, n_head)), acc=total, limit=12, name="total_far"
    )
    piece = width // PIECES
    sums = [total[:, g * piece : (g + 1) * piece] for g in range(PIECES)]
    far = []
    for bit in range(ctx_bits):
        last = bit == ctx_bits - 1
        got = [swap(s.astype(BF16), "ctx", 1 << bit, upward=last) for s in sums]
        if not last:
            sums = [s + g.astype(F32) for s, g in zip(sums, got)]
            present = (lax.axis_index("ctx") >> bit & 1).astype(BF16)
            got = [g * present for g in got]
        far += got

    queries, near = span_part(
        head, [tokens, tokens_c], far_x, value_weight, pair_weight, acc, mixing
    )
    weight_c = swap(output_weight, "head", 1)

    gain = out_gain.reshape(1, width)
    hidden, hidden_c, sent = [], [], []
    for c in range(CHUNKS):
        hid = hidden_part(
            c, CHUNKS, queries, far, PIECES, mixing, near, gain, levels - ctx_bits
        )
        hid_c = swap(hid, "head", 1)
        hidden.append(hid)
        hidden_c.append(hid_c)
    arrived = []
    for mask in range(2, n_head, 2):
        for c in range(CHUNKS):
            part = out_part(
                head, [hidden[c]], [hidden_c[c]], output_weight, weight_c, mask, block, BF16
            )
            arrived.append(swap(part, "head", mask))
    own = out_part(head, hidden, hidden_c, output_weight, weight_c, 0, block, F32)
    return sum_part(own, arrived, CHUNKS)


def solution(mesh):
    return jax.shard_map(
        local,
        mesh=mesh,
        in_specs=(
            P("ctx", "head"),
            P(),
            P(None, "head"),
            P("head", None),
            P("ctx", None),
            P(None, None, "head"),
            P("head"),
        ),
        out_specs=P("ctx", "head"),
        check_vma=False,
    )
```

```python
import functools
import math

import jax
import jax.numpy as jnp
from jax import lax
from jax.experimental import pallas as pl
from jax.experimental.pallas import tpu as pltpu
from jax.sharding import PartitionSpec as P


DH = 128
DK = 128
SPAN = 128
EPS = 1e-06
MIB = 1 << 20


F32 = jnp.float32
BF16 = jnp.bfloat16


def swap(value, axis, mask, upward=False):
    pairs = [(s, s ^ mask) for s in range(lax.axis_size(axis)) if not (upward and s & mask)]
    return lax.ppermute(value, axis, pairs)


def from_hbm(value):
    return pltpu.with_memory_space_constraint(value, pltpu.HBM)


def from_vmem(value):
    return pltpu.with_memory_space_constraint(value, pltpu.VMEM)


def fetch_kernel(picks, *refs):
    n = len(picks)
    head = lax.axis_index("head")
    sems = refs[-1]
    copies = []
    for a, (axis, size, offsets) in enumerate(picks):
        src, dst = refs[a], refs[n + a]
        for k, e in enumerate(offsets):
            start = pl.multiple_of((head ^ e) * size, size)
            view = src.at[pl.ds(start, size)] if axis == 0 else src.at[:, pl.ds(start, size)]
            rows = size if axis == 0 else src.shape[0]
            copies.append(
                pltpu.make_async_copy(view, dst.at[k * rows : (k + 1) * rows], sems.at[len(copies)])
            )
    for copy in copies:
        copy.start()
    for copy in copies:
        copy.wait()


def fetch(*picks):
    n = len(picks)
    out_shape = []
    for a, axis, size, offsets in picks:
        shape = (size, a.shape[1]) if axis == 0 else (a.shape[0], size)
        out_shape.append(pltpu.VMEM((shape[0] * len(offsets), shape[1]), a.dtype))
    copies = sum(len(p[3]) for p in picks)
    return pl.pallas_call(
        functools.partial(fetch_kernel, [p[1:] for p in picks]),
        out_shape=tuple(out_shape),
        in_specs=[pl.BlockSpec(memory_space=pl.ANY)] * n,
        out_specs=(pl.BlockSpec(memory_space=pltpu.VMEM),) * n,
        scratch_shapes=[pltpu.SemaphoreType.DMA((copies,))],
        compiler_params=params(1),
        cost_estimate=cost(0, 8 * MIB),
        name="fetch",
    )(*[p[0] for p in picks])


def unit_rows(values):
    scale = lax.rsqrt(jnp.mean(values * values, axis=-1, keepdims=True) + EPS)
    return values * scale / math.sqrt(values.shape[-1])


def mm(a, b):
    return jnp.dot(a, b, preferred_element_type=F32)


def mm_t(a, b):
    return lax.dot_general(a, b, (((0,), (0,)), ((), ())), preferred_element_type=F32)


def params(limit):
    return pltpu.CompilerParams(vmem_limit_bytes=limit * MIB)


def cost(flops, nbytes):
    return pl.CostEstimate(flops=flops, bytes_accessed=nbytes, transcendentals=0)


def full(shape):
    return pl.BlockSpec(shape, lambda *_: (0,) * len(shape))


def key_part_kernel(x_ref, w_ref, out_ref, *refs):
    kept, (w, sems) = refs[:-2], refs[-2:]
    feat = x_ref.shape[1]
    start = pl.multiple_of(lax.axis_index("head") * feat, feat)
    copies = [
        pltpu.make_async_copy(w_ref.at[pl.ds(start, feat), pl.ds(DK, DK)], w, sems.at[len(kept)])
    ]
    for c, ref in enumerate(kept):
        at = pl.ds(c * SPAN, SPAN)
        copies.append(pltpu.make_async_copy(x_ref.at[at], ref, sems.at[c]))
    for copy in copies:
        copy.start()
    copies[0].wait()
    for c, ref in enumerate(kept):
        copies[1 + c].wait()
        out_ref[c * SPAN : (c + 1) * SPAN] = mm(ref[...], w[...]).astype(BF16)


def key_part(tokens, pair_weight):
    rows, feat = tokens.shape
    spans = rows // SPAN
    return pl.pallas_call(
        key_part_kernel,
        out_shape=(jax.ShapeDtypeStruct((rows, DK), BF16),)
        + (pltpu.VMEM((SPAN, feat), BF16),) * spans,
        in_specs=[pl.BlockSpec(memory_space=pltpu.HBM)] * 2,
        out_specs=(pl.BlockSpec(memory_space=pltpu.VMEM),) * (1 + spans),
        scratch_shapes=[pltpu.VMEM((feat, DK), BF16), pltpu.SemaphoreType.DMA((1 + spans,))],
        compiler_params=params(4),
        cost_estimate=cost(2 * rows * feat * DK, 2 * rows * feat),
        name="key_part",
    )(from_hbm(tokens), from_hbm(pair_weight))


def key_tokens_kernel(n, *refs):
    part_refs, x_refs, out_ref = refs[:n], refs[n:-1], refs[-1]
    total = part_refs[0][...].astype(F32)
    for ref in part_refs[1:]:
        total = total + ref[...].astype(F32)
    keys = unit_rows(total).astype(BF16)
    out = None
    for c, ref in enumerate(x_refs):
        part = mm_t(keys[c * SPAN : (c + 1) * SPAN], ref[...])
        out = part if out is None else out + part
    out_ref[...] = out.astype(BF16)


def key_tokens(parts, kept):
    feat = kept[0].shape[1]
    return pl.pallas_call(
        functools.partial(key_tokens_kernel, len(parts)),
        out_shape=jax.ShapeDtypeStruct((DK, feat), BF16),
        compiler_params=params(4),
        cost_estimate=cost(2 * SPAN * len(kept) * feat * DK, 2 * SPAN * len(kept) * feat),
        name="key_tokens",
    )(*parts, *[from_vmem(k) for k in kept])


def mix_kernel(ctx_bits, index_ref, table_ref, out_ref, wide):
    levels, heads, size = table_ref.shape
    ctx = lax.axis_index("ctx")
    wide[...] = jnp.zeros_like(wide)
    hot = []
    for l in range(levels):
        table = table_ref[l]
        bit = l - (levels - ctx_bits)
        if bit >= 0:
            table = table * ((ctx >> bit) & 1).astype(F32)
        wide[l * heads : (l + 1) * heads, l * size : (l + 1) * size] = table
        ids = lax.broadcasted_iota(jnp.int32, (size, index_ref.shape[1]), 0)
        hot.append((ids == index_ref[l : l + 1, :]).astype(F32))
    hot = jnp.concatenate(hot, axis=0).astype(BF16)
    rest = wide[...]
    total = None
    for _ in range(3):
        part = rest.astype(BF16)
        rest = rest - part.astype(F32)
        value = lax.dot_general(hot, part, (((0,), (1,)), ((), ())), preferred_element_type=F32)
        total = value if total is None else total + value
    out_ref[...] = total


def mix_part(level_index, level_table, ctx_bits):
    rows = level_index.shape[0]
    levels, size, heads = level_table.shape
    return pl.pallas_call(
        functools.partial(mix_kernel, ctx_bits),
        out_shape=jax.ShapeDtypeStruct((rows, levels * heads), F32),
        scratch_shapes=[pltpu.VMEM((levels * heads, levels * size), F32)],
        compiler_params=params(4),
        cost_estimate=cost(6 * rows * levels * levels * heads * size, 4 * rows * levels * heads),
        name="mix_part",
    )(level_index.T, level_table.transpose(0, 2, 1))


def near_kernel(*refs):
    kept, (x1, w_ref, p_ref, vals_ref, pair_ref, x0) = refs[:-6], refs[-6:]
    feat = x0.shape[1]
    for c, ref in enumerate(kept):
        x0[c * SPAN : (c + 1) * SPAN] = ref[...]
    vals_ref[...] = mm(x0[...], w_ref[:feat]) + mm(x1[...], w_ref[feat:])
    pair_ref[...] = mm(x0[...], p_ref[:feat]) + mm(x1[...], p_ref[feat:])


def near_part(kept, tokens_c, weight, pair_weight):
    rows, feat = tokens_c.shape
    width = weight.shape[1]
    return pl.pallas_call(
        near_kernel,
        out_shape=(
            jax.ShapeDtypeStruct((rows, width), F32),
            jax.ShapeDtypeStruct((rows, 2 * DK), F32),
        ),
        scratch_shapes=[pltpu.VMEM((rows, feat), BF16)],
        compiler_params=params(6),
        cost_estimate=cost(4 * rows * feat * width, 4 * feat * width),
        name="near_part",
    )(*[from_vmem(k) for k in kept], tokens_c, from_vmem(weight), from_vmem(pair_weight))


def total_kernel(n, has_acc, *refs):
    lhs = refs[:n]
    w_ref = refs[n]
    feat = lhs[0].shape[1]
    total = refs[n + 1][...] if has_acc else None
    for e in range(n):
        part = mm(lhs[e][...], w_ref[e * feat : (e + 1) * feat])
        total = part if total is None else total + part
    if has_acc:
        outs = refs[n + 2 :]
        piece = outs[0].shape[1]
        for g, ref in enumerate(outs):
            ref[...] = total[:, g * piece : (g + 1) * piece].astype(BF16)
    else:
        refs[-1][...] = total


def total_part(lhs, weight, acc=None, pieces=1):
    rows, feat = lhs[0].shape
    width = weight.shape[1]
    n = len(lhs)
    operands = [*lhs, from_vmem(weight)]
    if acc is None:
        out_shape = jax.ShapeDtypeStruct((rows, width), F32)
    else:
        operands.append(acc)
        out_shape = (jax.ShapeDtypeStruct((rows, width // pieces), BF16),) * pieces
    return pl.pallas_call(
        functools.partial(total_kernel, n, acc is not None),
        out_shape=out_shape,
        compiler_params=params(8),
        cost_estimate=cost(2 * rows * feat * width * n, 2 * n * feat * width),
        name="total_part",
    )(*operands)


def add_kernel(a_ref, b_ref, out_ref):
    out_ref[...] = (a_ref[...].astype(F32) + b_ref[...].astype(F32)).astype(BF16)


def add_part(a, b):
    return pl.pallas_call(
        add_kernel,
        out_shape=jax.ShapeDtypeStruct(a.shape, BF16),
        compiler_params=params(2),
        cost_estimate=cost(a.size, 6 * a.size),
        name="add_part",
    )(a, b)


def needed(span, bits):
    tops = [(span >> b << b, 1 << b) for b in range(bits) if span >> b & 1]
    return [list(range(top - size, top)) for top, size in tops]


def span_kernel(span, bits, n_far, keep, *refs):
    far = refs[:n_far]
    w_ref, p_ref, v0_ref, p0_ref, mix_ref = refs[n_far : n_far + 5]
    buckets = needed(span, bits)
    first = min((j for js in buckets for j in js), default=span)
    states = {j: refs[n_far + 5 + j - first] for j in range(first, span)}
    outs = refs[n_far + 5 + span - first :]
    q_ref, out_ref = outs[0], outs[1]
    feat = far[0].shape[1]
    heads = out_ref.shape[1] // DH
    vals, pair = v0_ref[...], p0_ref[...]
    for e in range(n_far):
        at = slice(e * feat, (e + 1) * feat)
        vals = vals + mm(far[e][...], w_ref[at])
        pair = pair + mm(far[e][...], p_ref[at])
    queries = unit_rows(pair[:, :DK]).astype(BF16)
    keys = unit_rows(pair[:, DK:]).astype(BF16)
    vals = vals.astype(BF16)
    q_ref[...] = queries
    causal = (
        lax.broadcasted_iota(jnp.int32, (SPAN, SPAN), 0)
        >= lax.broadcasted_iota(jnp.int32, (SPAN, SPAN), 1)
    )
    scores = lax.dot_general(queries, keys, (((1,), (1,)), ((), ())), preferred_element_type=F32)
    scores = jnp.where(causal, scores, 0.0).astype(BF16)
    reads = [(0, mm(scores, vals))]
    levels = [1 + b for b in range(bits) if span >> b & 1]
    for level, js in zip(levels, buckets):
        bucket = states[js[0]][...]
        for j in js[1:]:
            bucket = bucket + states[j][...]
        reads.append((level, mm(queries, bucket.astype(BF16))))
    if keep:
        outs[2][...] = mm_t(keys, vals)
    for h in range(heads):
        cols = slice(h * DH, (h + 1) * DH)
        total = None
        for level, value in reads:
            col = level * heads + h
            part = value[:, cols] * mix_ref[:, col : col + 1]
            total = part if total is None else total + part
        out_ref[:, cols] = total


def span_part(span, spans, far, weight, pair_weight, vals, pair, mixing, states):
    rows, feat = far[0].shape
    width = weight.shape[1]
    bits = spans.bit_length() - 1
    n_far = len(far)
    first = min((j for js in needed(span, bits) for j in js), default=span)
    prior = states[first:span]
    keep = span < spans - 1

    def block(cols):
        return pl.BlockSpec((rows, cols), lambda i: (span, 0))

    def whole(value):
        return pl.BlockSpec(value.shape, lambda i: (0, 0))

    out_shape = [
        jax.ShapeDtypeStruct((rows, DK), BF16),
        jax.ShapeDtypeStruct((rows, width), F32),
    ]
    if keep:
        out_shape.append(jax.ShapeDtypeStruct((DK, width), F32))
    out = pl.pallas_call(
        functools.partial(span_kernel, span, bits, n_far, keep),
        out_shape=out_shape,
        grid=(1,),
        in_specs=[whole(f) for f in far]
        + [pl.BlockSpec(memory_space=pltpu.VMEM)] * 2
        + [block(width), block(2 * DK), block(mixing.shape[1])]
        + [whole(p) for p in prior],
        out_specs=[whole(o) for o in out_shape],
        compiler_params=params(16),
        cost_estimate=cost(2 * rows * feat * width * n_far, 2 * n_far * feat * width),
        name="span_part",
    )(*far, from_vmem(weight), from_vmem(pair_weight), vals, pair, mixing, *prior)
    return out[0], out[1], (out[2] if keep else None)


def hidden_kernel(n_far, pieces, first_level, q_ref, *refs):
    far = refs[: n_far * pieces]
    mix_ref, near_ref, gain_ref, out_ref = refs[n_far * pieces :]
    width = out_ref.shape[1]
    heads = width // DH
    per = heads // pieces
    for h in range(heads):
        cols = slice(h * DH, (h + 1) * DH)
        total = near_ref[:, cols]
        g, k = divmod(h, per)
        for b in range(n_far):
            col = (first_level + b) * heads + h
            value = mm(q_ref[...], far[b * pieces + g][:, k * DH : (k + 1) * DH])
            total = total + value * mix_ref[:, col : col + 1]
        scale = lax.rsqrt(jnp.mean(total * total, axis=-1, keepdims=True) + EPS)
        out_ref[:, cols] = (total * scale * gain_ref[:, cols]).astype(BF16)


def hidden_part(i, queries, far, pieces, mixing, near, gain, first_level):
    size, width = near.shape
    n_far = len(far) // pieces

    return pl.pallas_call(
        functools.partial(hidden_kernel, n_far, pieces, first_level),
        out_shape=jax.ShapeDtypeStruct((size, width), BF16),
        grid=(1,),
        in_specs=[full((size, DK))]
        + [full(f.shape) for f in far]
        + [
            pl.BlockSpec((size, mixing.shape[1]), lambda k: (i, 0)),
            full((size, width)),
            full((1, width)),
        ],
        out_specs=full((size, width)),
        compiler_params=params(12),
        cost_estimate=cost(2 * size * DK * width * n_far, 6 * size * width),
        name="hidden_part",
    )(queries, *far, mixing, near, gain)


def out_kernel(own_ref, other_ref, w_ref, v_ref, out_ref):
    out = mm(own_ref[...], w_ref[...]) + mm(other_ref[...], v_ref[...])
    out_ref[...] = out.astype(BF16)


def out_part(own, other, weight, weight_other):
    size, width = own.shape
    block = weight.shape[1]
    return pl.pallas_call(
        out_kernel,
        out_shape=jax.ShapeDtypeStruct((size, block), BF16),
        compiler_params=params(8),
        cost_estimate=cost(4 * size * width * block, 4 * width * block),
        name="out_part",
    )(own, other, from_vmem(weight), from_vmem(weight_other))


def own_kernel(chunks, *refs):
    own, other = refs[:chunks], refs[chunks : 2 * chunks]
    w_ref, v_ref, out_ref, xa, xb = refs[2 * chunks :]
    size = own[0].shape[0]
    for c in range(chunks):
        xa[c * size : (c + 1) * size] = own[c][...]
        xb[c * size : (c + 1) * size] = other[c][...]
    out_ref[...] = mm(xa[...], w_ref[...]) + mm(xb[...], v_ref[...])


def own_part(own, other, weight, weight_other):
    chunks = len(own)
    size, width = own[0].shape
    block = weight.shape[1]
    return pl.pallas_call(
        functools.partial(own_kernel, chunks),
        out_shape=jax.ShapeDtypeStruct((size * chunks, block), F32),
        scratch_shapes=[pltpu.VMEM((size * chunks, width), BF16)] * 2,
        compiler_params=params(6),
        cost_estimate=cost(4 * size * chunks * width * block, 4 * width * block),
        name="own_part",
    )(*own, *other, from_vmem(weight), from_vmem(weight_other))


def sum_kernel(chunks, acc_ref, *refs):
    out_ref = refs[-1]
    size = out_ref.shape[0] // chunks
    for c in range(chunks):
        at = slice(c * size, (c + 1) * size)
        total = acc_ref[at]
        for ref in refs[c:-1:chunks]:
            total = total + ref[...].astype(F32)
        out_ref[at] = total.astype(BF16)


def sum_part(acc, arrived, chunks):
    return pl.pallas_call(
        functools.partial(sum_kernel, chunks),
        out_shape=jax.ShapeDtypeStruct(acc.shape, BF16),
        compiler_params=params(12),
        cost_estimate=cost(acc.size, 8 * acc.size),
        name="sum_part",
    )(acc, *arrived)


PIECES = 2


def local(tokens, pair_weight, value_weight, output_weight, level_index, level_table, out_gain):
    rows = tokens.shape[0]
    width = value_weight.shape[1]
    n_head = lax.axis_size("head")
    n_ctx = lax.axis_size("ctx")
    ctx_bits = n_ctx.bit_length() - 1
    levels = level_table.shape[0]
    spans = rows // SPAN
    block = output_weight.shape[1] // n_head
    masks = range(2, n_head, 2)

    feat = tokens.shape[1]
    near_at, far_at = (0, 1), tuple(range(2, n_head))

    own_key, *kept = key_part(tokens, pair_weight)
    parts = [own_key, swap(own_key, "head", 1)]
    for mask in masks:
        got = swap(own_key, "head", mask)
        parts += [got, swap(got, "head", 1)]

    mixing = mix_part(level_index, level_table, ctx_bits)

    tokens_c = swap(tokens, "head", 1)
    far_x = []
    for c in range(spans):
        far = []
        for mask in masks:
            got = swap(kept[c], "head", mask)
            far += [got, swap(got, "head", 1)]
        far_x.append(far)

    w_near, p_near = fetch(
        (from_hbm(value_weight), 0, feat, near_at), (from_hbm(pair_weight), 0, feat, near_at)
    )
    kx = key_tokens(parts, kept)
    kx_c = swap(kx, "head", 1)
    kx_far = []
    for mask in masks:
        got = swap(kx, "head", mask)
        kx_far += [got, swap(got, "head", 1)]
    total = total_part([kx, kx_c], w_near)
    vals, pair = near_part(kept, tokens_c, w_near, p_near)
    w_far, p_far = fetch((from_hbm(value_weight), 0, feat, far_at), (from_hbm(pair_weight), 0, feat, far_at))
    sums = total_part(kx_far, w_far, total, PIECES)

    far = []
    for bit in range(ctx_bits):
        last = bit == ctx_bits - 1
        got = [swap(s, "ctx", 1 << bit, upward=False) for s in sums]
        if not last:
            sums = [add_part(s, g) for s, g in zip(sums, got)]
        far += got

    weight_c = swap(output_weight, "head", 1)

    queries, near, states = [], [], []
    for c in range(spans):
        q, part, state = span_part(
            c, spans, far_x[c], w_far, p_far, vals, pair, mixing, states
        )
        queries.append(q)
        near.append(part)
        states.append(state)

    gain = out_gain.reshape(1, width)
    hidden, hidden_c = [], []
    for c in range(spans):
        hid = hidden_part(
            c, queries[c], far, PIECES, mixing, near[c], gain, levels - ctx_bits
        )
        hidden.append(hid)
        hidden_c.append(swap(hid, "head", 1))
    arrived = []
    for mask in masks:
        w_own, w_other = fetch(
            (from_hbm(output_weight), 1, block, (mask,)), (weight_c, 1, block, (mask,))
        )
        for c in range(spans):
            part = out_part(hidden[c], hidden_c[c], w_own, w_other)
            arrived.append(swap(part, "head", mask))
    w_own, w_other = fetch((from_hbm(output_weight), 1, block, (0,)), (weight_c, 1, block, (0,)))
    own = own_part(hidden, hidden_c, w_own, w_other)
    return sum_part(own, arrived, spans)


def solution(mesh):
    return jax.shard_map(
        local,
        mesh=mesh,
        in_specs=(
            P("ctx", "head"),
            P(),
            P(None, "head"),
            P("head", None),
            P("ctx", None),
            P(None, None, "head"),
            P("head"),
        ),
        out_specs=P("ctx", "head"),
        check_vma=False,
    )
```

```python
import functools
import math

import jax
import jax.numpy as jnp
from jax import lax
from jax.experimental import pallas as pl
from jax.experimental.pallas import tpu as pltpu
from jax.sharding import PartitionSpec as P


DH = 128
DK = 128
SPAN = 128
EPS = 1e-06
MIB = 1 << 20


F32 = jnp.float32
BF16 = jnp.bfloat16


def swap(value, axis, mask):
    pairs = [(s, s ^ mask) for s in range(lax.axis_size(axis))]
    return lax.ppermute(value, axis, pairs)


def from_hbm(value):
    return pltpu.with_memory_space_constraint(value, pltpu.HBM)


def from_vmem(value):
    return pltpu.with_memory_space_constraint(value, pltpu.VMEM)


def block_copies(picks, sources, targets, sems):
    head = lax.axis_index("head")
    copies = []
    for (axis, size, offsets), src, dst in zip(picks, sources, targets):
        for k, e in enumerate(offsets):
            start = pl.multiple_of((head ^ e) * size, size)
            view = src.at[pl.ds(start, size)] if axis == 0 else src.at[:, pl.ds(start, size)]
            rows = size if axis == 0 else src.shape[0]
            copies.append(
                pltpu.make_async_copy(view, dst.at[k * rows : (k + 1) * rows], sems.at[len(copies)])
            )
    return copies


def block_shapes(picks):
    shapes = []
    for a, axis, size, offsets in picks:
        shape = (size, a.shape[1]) if axis == 0 else (a.shape[0], size)
        shapes.append(pltpu.VMEM((shape[0] * len(offsets), shape[1]), a.dtype))
    return tuple(shapes)


def fetch_kernel(picks, *refs):
    n = len(picks)
    copies = block_copies(picks, refs[:n], refs[n:-1], refs[-1])
    for copy in copies:
        copy.start()
    for copy in copies:
        copy.wait()


def fetch(*picks):
    n = len(picks)
    copies = sum(len(p[3]) for p in picks)
    return pl.pallas_call(
        functools.partial(fetch_kernel, [p[1:] for p in picks]),
        out_shape=block_shapes(picks),
        in_specs=[pl.BlockSpec(memory_space=pl.ANY)] * n,
        out_specs=(pl.BlockSpec(memory_space=pltpu.VMEM),) * n,
        scratch_shapes=[pltpu.SemaphoreType.DMA((copies,))],
        compiler_params=params(1),
        cost_estimate=cost(0, 8 * MIB),
        name="fetch",
    )(*[p[0] for p in picks])


def unit_rows(values):
    scale = lax.rsqrt(jnp.mean(values * values, axis=-1, keepdims=True) + EPS)
    return values * scale / math.sqrt(values.shape[-1])


def mm(a, b):
    return jnp.dot(a, b, preferred_element_type=F32)


def mm_t(a, b):
    return lax.dot_general(a, b, (((0,), (0,)), ((), ())), preferred_element_type=F32)


def params(limit):
    return pltpu.CompilerParams(vmem_limit_bytes=limit * MIB)


def cost(flops, nbytes):
    return pl.CostEstimate(flops=flops, bytes_accessed=nbytes, transcendentals=0)


def full(shape):
    return pl.BlockSpec(shape, lambda *_: (0,) * len(shape))


def key_part_kernel(x_ref, w_ref, out_ref, *refs):
    kept, (w, sems) = refs[:-2], refs[-2:]
    feat = x_ref.shape[1]
    start = pl.multiple_of(lax.axis_index("head") * feat, feat)
    copies = [
        pltpu.make_async_copy(w_ref.at[pl.ds(start, feat), pl.ds(DK, DK)], w, sems.at[len(kept)])
    ]
    size = kept[0].shape[0]
    for c, ref in enumerate(kept):
        at = pl.ds(c * size, size)
        copies.append(pltpu.make_async_copy(x_ref.at[at], ref, sems.at[c]))
    for copy in copies:
        copy.start()
    copies[0].wait()
    for c, ref in enumerate(kept):
        copies[1 + c].wait()
        out_ref[c * size : (c + 1) * size] = mm(ref[...], w[...]).astype(BF16)


def key_part(tokens, pair_weight, chunks):
    rows, feat = tokens.shape
    return pl.pallas_call(
        key_part_kernel,
        out_shape=(jax.ShapeDtypeStruct((rows, DK), BF16),)
        + (pltpu.VMEM((rows // chunks, feat), BF16),) * chunks,
        in_specs=[pl.BlockSpec(memory_space=pltpu.HBM)] * 2,
        out_specs=(pl.BlockSpec(memory_space=pltpu.VMEM),) * (1 + chunks),
        scratch_shapes=[pltpu.VMEM((feat, DK), BF16), pltpu.SemaphoreType.DMA((1 + chunks,))],
        compiler_params=params(4),
        cost_estimate=cost(2 * rows * feat * DK, 2 * rows * feat),
        name="key_part",
    )(from_hbm(tokens), from_hbm(pair_weight))


def key_tokens_kernel(n, *refs):
    part_refs, x_refs, out_ref = refs[:n], refs[n:-1], refs[-1]
    total = part_refs[0][...].astype(F32)
    for ref in part_refs[1:]:
        total = total + ref[...].astype(F32)
    keys = unit_rows(total).astype(BF16)
    out = None
    size = x_refs[0].shape[0]
    for c, ref in enumerate(x_refs):
        part = mm_t(keys[c * size : (c + 1) * size], ref[...])
        out = part if out is None else out + part
    out_ref[...] = out.astype(BF16)


def key_tokens(parts, kept):
    feat = kept[0].shape[1]
    return pl.pallas_call(
        functools.partial(key_tokens_kernel, len(parts)),
        out_shape=jax.ShapeDtypeStruct((DK, feat), BF16),
        compiler_params=params(4),
        cost_estimate=cost(2 * kept[0].size * len(kept) * DK, 2 * kept[0].size * len(kept)),
        name="key_tokens",
    )(*parts, *[from_vmem(k) for k in kept])


def mix_kernel(ctx_bits, index_ref, table_ref, out_ref, wide):
    levels, heads, size = table_ref.shape
    ctx = lax.axis_index("ctx")
    wide[...] = jnp.zeros_like(wide)
    hot = []
    for l in range(levels):
        table = table_ref[l]
        bit = l - (levels - ctx_bits)
        if bit >= 0:
            table = table * ((ctx >> bit) & 1).astype(F32)
        wide[l * heads : (l + 1) * heads, l * size : (l + 1) * size] = table
        ids = lax.broadcasted_iota(jnp.int32, (size, index_ref.shape[1]), 0)
        hot.append((ids == index_ref[l : l + 1, :]).astype(F32))
    hot = jnp.concatenate(hot, axis=0).astype(BF16)
    rest = wide[...]
    total = None
    for _ in range(3):
        part = rest.astype(BF16)
        rest = rest - part.astype(F32)
        value = lax.dot_general(hot, part, (((0,), (1,)), ((), ())), preferred_element_type=F32)
        total = value if total is None else total + value
    out_ref[...] = total


def mix_part(level_index, level_table, ctx_bits):
    rows = level_index.shape[0]
    levels, size, heads = level_table.shape
    return pl.pallas_call(
        functools.partial(mix_kernel, ctx_bits),
        out_shape=jax.ShapeDtypeStruct((rows, levels * heads), F32),
        scratch_shapes=[pltpu.VMEM((levels * heads, levels * size), F32)],
        compiler_params=params(4),
        cost_estimate=cost(6 * rows * levels * levels * heads * size, 4 * rows * levels * heads),
        name="mix_part",
    )(level_index.T, level_table.transpose(0, 2, 1))


def near_kernel(chunk, x0, x1, w_ref, p_ref, vals_ref, pair_ref):
    rows, feat = x0.shape
    a, b = x0[...], x1[chunk * rows : (chunk + 1) * rows]
    vals_ref[...] = mm(a, w_ref[:feat]) + mm(b, w_ref[feat:])
    pair_ref[...] = mm(a, p_ref[:feat]) + mm(b, p_ref[feat:])


def near_part(chunk, kept, tokens_c, weight, pair_weight):
    rows, feat = kept.shape
    width = weight.shape[1]
    return pl.pallas_call(
        functools.partial(near_kernel, chunk),
        out_shape=(
            jax.ShapeDtypeStruct((rows, width), F32),
            jax.ShapeDtypeStruct((rows, 2 * DK), F32),
        ),
        compiler_params=params(6),
        cost_estimate=cost(4 * rows * feat * width, 4 * feat * width),
        name="near_part",
    )(from_vmem(kept), tokens_c, from_vmem(weight), from_vmem(pair_weight))


def total_kernel(n, has_acc, *refs):
    lhs = refs[:n]
    w_ref = refs[n]
    feat = lhs[0].shape[1]
    total = refs[n + 1][...] if has_acc else None
    for e in range(n):
        part = mm(lhs[e][...], w_ref[e * feat : (e + 1) * feat])
        total = part if total is None else total + part
    if has_acc:
        start = 0
        for ref in refs[n + 2 :]:
            stop = start + ref.shape[1]
            ref[...] = total[:, start:stop].astype(BF16)
            start = stop
    else:
        refs[-1][...] = total


def total_part(lhs, weight, acc=None, pieces=()):
    rows, feat = lhs[0].shape
    width = weight.shape[1]
    n = len(lhs)
    operands = [*lhs, from_vmem(weight)]
    if acc is None:
        out_shape = jax.ShapeDtypeStruct((rows, width), F32)
    else:
        operands.append(acc)
        out_shape = tuple(jax.ShapeDtypeStruct((rows, p), BF16) for p in pieces)
    return pl.pallas_call(
        functools.partial(total_kernel, n, acc is not None),
        out_shape=out_shape,
        compiler_params=params(8),
        cost_estimate=cost(2 * rows * feat * width * n, 2 * n * feat * width),
        name="total_part",
    )(*operands)


def add_kernel(a_ref, b_ref, out_ref):
    out_ref[...] = (a_ref[...].astype(F32) + b_ref[...].astype(F32)).astype(BF16)


def add_part(a, b):
    return pl.pallas_call(
        add_kernel,
        out_shape=jax.ShapeDtypeStruct(a.shape, BF16),
        compiler_params=params(2),
        cost_estimate=cost(a.size, 6 * a.size),
        name="add_part",
    )(a, b)


def head_places(pieces):
    return [(g, slice(k * DH, (k + 1) * DH)) for g, p in enumerate(pieces) for k in range(p // DH)]


def needed(span, bits):
    tops = [(span >> b << b, 1 << b) for b in range(bits) if span >> b & 1]
    return [list(range(top - size, top)) for top, size in tops]


def span_kernel(span, row, bits, n_far, keep, pieces, n_remote, *refs):
    far = refs[:n_far]
    w_ref, p_ref, v0_ref, p0_ref, mix_ref = refs[n_far : n_far + 5]
    buckets = needed(span, bits)
    first = min((j for js in buckets for j in js), default=span)
    states = {j: refs[n_far + 5 + j - first] for j in range(first, span)}
    remote = refs[n_far + 5 + span - first :]
    outs = remote[n_remote:]
    q_ref, out_ref = outs[0], outs[1]
    feat = far[0].shape[1]
    heads = out_ref.shape[1] // DH
    rows = slice(row, row + SPAN)
    vals, pair = v0_ref[rows], p0_ref[rows]
    for e in range(n_far):
        at = slice(e * feat, (e + 1) * feat)
        x = far[e][rows]
        vals = vals + mm(x, w_ref[at])
        pair = pair + mm(x, p_ref[at])
    queries = unit_rows(pair[:, :DK]).astype(BF16)
    keys = unit_rows(pair[:, DK:]).astype(BF16)
    vals = vals.astype(BF16)
    q_ref[...] = queries
    causal = (
        lax.broadcasted_iota(jnp.int32, (SPAN, SPAN), 0)
        >= lax.broadcasted_iota(jnp.int32, (SPAN, SPAN), 1)
    )
    scores = lax.dot_general(queries, keys, (((1,), (1,)), ((), ())), preferred_element_type=F32)
    scores = jnp.where(causal, scores, 0.0).astype(BF16)
    reads = [(0, mm(scores, vals))]
    levels = [1 + b for b in range(bits) if span >> b & 1]
    for level, js in zip(levels, buckets):
        bucket = states[js[0]][...]
        for j in js[1:]:
            bucket = bucket + states[j][...]
        reads.append((level, mm(queries, bucket.astype(BF16))))
    if keep:
        outs[2][...] = mm_t(keys, vals)
    places = head_places(pieces)
    for h in range(heads):
        cols = slice(h * DH, (h + 1) * DH)
        total = None
        for level, value in reads:
            col = level * heads + h
            part = value[:, cols] * mix_ref[:, col : col + 1]
            total = part if total is None else total + part
        g, at = places[h]
        for b in range(n_remote // len(pieces)):
            col = (1 + bits + b) * heads + h
            value = mm(queries, remote[b * len(pieces) + g][:, at])
            total = total + value * mix_ref[:, col : col + 1]
        out_ref[:, cols] = total


def span_part(span, spans, far, weight, pair_weight, vals, pair, mixing, states, pieces, remote):
    feat = far[0].shape[1]
    width = weight.shape[1]
    bits = spans.bit_length() - 1
    n_far = len(far)
    first = min((j for js in needed(span, bits) for j in js), default=span)
    prior = states[first:span]
    keep = span < spans - 1
    row = span * SPAN % far[0].shape[0]

    def whole(value):
        return pl.BlockSpec(value.shape, lambda i: (0, 0))

    out_shape = [
        jax.ShapeDtypeStruct((SPAN, DK), BF16),
        jax.ShapeDtypeStruct((SPAN, width), F32),
    ]
    if keep:
        out_shape.append(jax.ShapeDtypeStruct((DK, width), F32))
    vmem = pl.BlockSpec(memory_space=pltpu.VMEM)
    out = pl.pallas_call(
        functools.partial(span_kernel, span, row, bits, n_far, keep, pieces, len(remote)),
        out_shape=out_shape,
        grid=(1,),
        in_specs=[vmem] * (n_far + 4)
        + [pl.BlockSpec((SPAN, mixing.shape[1]), lambda i: (span, 0))]
        + [whole(p) for p in [*prior, *remote]],
        out_specs=[whole(o) for o in out_shape],
        compiler_params=params(6),
        cost_estimate=cost(2 * SPAN * feat * width * n_far, 2 * n_far * feat * width),
        name="span_part",
    )(*far, from_vmem(weight), from_vmem(pair_weight), vals, pair, mixing, *prior, *remote)
    return out[0], out[1], (out[2] if keep else None)


def hidden_kernel(pieces, level, q_ref, *refs):
    last = refs[: len(pieces)]
    mix_ref, near_ref, gain_ref, out_ref = refs[len(pieces) :]
    heads = out_ref.shape[1] // DH
    for h, (g, at) in enumerate(head_places(pieces)):
        cols = slice(h * DH, (h + 1) * DH)
        col = level * heads + h
        value = mm(q_ref[...], last[g][:, at])
        total = near_ref[:, cols] + value * mix_ref[:, col : col + 1]
        scale = lax.rsqrt(jnp.mean(total * total, axis=-1, keepdims=True) + EPS)
        out_ref[:, cols] = (total * scale * gain_ref[:, cols]).astype(BF16)


def hidden_part(chunk, queries, last, pieces, mixing, near, gain, level):
    span, start, size = chunk
    width = near.shape[1]

    def rows(cols):
        return pl.BlockSpec((size, cols), lambda k: (start // size, 0))

    return pl.pallas_call(
        functools.partial(hidden_kernel, pieces, level),
        out_shape=jax.ShapeDtypeStruct((size, width), BF16),
        grid=(1,),
        in_specs=[rows(DK)]
        + [full(f.shape) for f in last]
        + [
            pl.BlockSpec((size, mixing.shape[1]), lambda k: ((span * SPAN + start) // size, 0)),
            rows(width),
            full((1, width)),
        ],
        out_specs=full((size, width)),
        compiler_params=params(4),
        cost_estimate=cost(2 * size * DK * width, 6 * size * width),
        name="hidden_part",
    )(queries, *last, mixing, near, gain)


def out_kernel(own_ref, other_ref, w_ref, v_ref, out_ref):
    out = mm(own_ref[...], w_ref[...]) + mm(other_ref[...], v_ref[...])
    out_ref[...] = out.astype(BF16)


def out_part(own, other, weight, weight_other):
    size, width = own.shape
    block = weight.shape[1]
    return pl.pallas_call(
        out_kernel,
        out_shape=jax.ShapeDtypeStruct((size, block), BF16),
        compiler_params=params(8),
        cost_estimate=cost(4 * size * width * block, 4 * width * block),
        name="out_part",
    )(own, other, from_vmem(weight), from_vmem(weight_other))


def own_kernel(chunks, *refs):
    own, other = refs[:chunks], refs[chunks : 2 * chunks]
    w_ref, v_ref, out_ref, xa, xb = refs[2 * chunks :]
    start = 0
    for a, b in zip(own, other):
        stop = start + a.shape[0]
        xa[start:stop] = a[...]
        xb[start:stop] = b[...]
        start = stop
    out_ref[...] = mm(xa[...], w_ref[...]) + mm(xb[...], v_ref[...])


def own_part(own, other, weight, weight_other):
    rows = sum(a.shape[0] for a in own)
    width = own[0].shape[1]
    block = weight.shape[1]
    return pl.pallas_call(
        functools.partial(own_kernel, len(own)),
        out_shape=jax.ShapeDtypeStruct((rows, block), F32),
        scratch_shapes=[pltpu.VMEM((rows, width), BF16)] * 2,
        compiler_params=params(6),
        cost_estimate=cost(4 * rows * width * block, 4 * width * block),
        name="own_part",
    )(*own, *other, from_vmem(weight), from_vmem(weight_other))


def sum_kernel(chunks, acc_ref, *refs):
    arrived, out_ref, stage, sem = refs[:-3], refs[-3], refs[-2], refs[-1]
    start = 0
    for c in range(chunks):
        stop = start + arrived[c].shape[0]
        total = acc_ref[start:stop]
        for ref in arrived[c::chunks]:
            total = total + ref[...].astype(F32)
        stage[start:stop] = total.astype(BF16)
        start = stop
    copy = pltpu.make_async_copy(stage, out_ref.at[0:start], sem)
    copy.start()
    copy.wait()


def sum_part(acc, arrived, chunks):
    rows = sum(a.shape[0] for a in arrived[:chunks])
    vmem = pl.BlockSpec(memory_space=pltpu.VMEM)
    return pl.pallas_call(
        functools.partial(sum_kernel, chunks),
        out_shape=jax.ShapeDtypeStruct(acc.shape, BF16),
        in_specs=[vmem] * (1 + len(arrived)),
        out_specs=pl.BlockSpec(memory_space=pl.ANY),
        scratch_shapes=[pltpu.VMEM((rows, acc.shape[1]), BF16), pltpu.SemaphoreType.DMA(())],
        compiler_params=params(4),
        cost_estimate=cost(acc.size, 8 * acc.size),
        name="sum_part",
    )(acc, *arrived)


def last_kernel(n, acc_ref, done_ref, *refs):
    arrived, (out_ref, stage, sem) = refs[:n], refs[n:]
    rows = stage.shape[0]
    total = acc_ref[-rows:]
    for ref in arrived:
        total = total + ref[...].astype(F32)
    stage[...] = total.astype(BF16)
    copy = pltpu.make_async_copy(stage, out_ref.at[out_ref.shape[0] - rows :], sem)
    copy.start()
    copy.wait()


def last_part(acc, done, arrived):
    rows = arrived[0].shape[0]
    vmem = pl.BlockSpec(memory_space=pltpu.VMEM)
    hbm = pl.BlockSpec(memory_space=pl.ANY)
    return pl.pallas_call(
        functools.partial(last_kernel, len(arrived)),
        out_shape=jax.ShapeDtypeStruct(acc.shape, BF16),
        in_specs=[vmem, hbm] + [vmem] * len(arrived),
        out_specs=hbm,
        input_output_aliases={1: 0},
        scratch_shapes=[pltpu.VMEM((rows, acc.shape[1]), BF16), pltpu.SemaphoreType.DMA(())],
        compiler_params=params(2),
        cost_estimate=cost(acc.size, 2 * acc.size),
        name="last_part",
    )(acc, done, *arrived)


PARTS = (3, 5)
GROUPS = 2
FIRST = 1


def local(tokens, pair_weight, value_weight, output_weight, level_index, level_table, out_gain):
    rows = tokens.shape[0]
    width = value_weight.shape[1]
    n_head = lax.axis_size("head")
    n_ctx = lax.axis_size("ctx")
    ctx_bits = n_ctx.bit_length() - 1
    levels = level_table.shape[0]
    spans = rows // SPAN
    block = output_weight.shape[1] // n_head
    masks = range(2, n_head, 2)

    feat = tokens.shape[1]
    near_at, far_at = (0, 1), tuple(range(2, n_head))

    own_key, *kept = key_part(tokens, pair_weight, GROUPS)
    parts = [own_key, swap(own_key, "head", 1)]
    for mask in masks:
        got = swap(own_key, "head", mask)
        parts += [got, swap(got, "head", 1)]

    mixing = mix_part(level_index, level_table, ctx_bits)

    tokens_c = swap(tokens, "head", 1)
    far_x = []
    for c in range(GROUPS):
        far = []
        for mask in masks:
            got = swap(kept[c], "head", mask)
            far += [got, swap(got, "head", 1)]
        far_x.append(far)

    w_near, p_near = fetch(
        (from_hbm(value_weight), 0, feat, near_at), (from_hbm(pair_weight), 0, feat, near_at)
    )
    kx = key_tokens(parts, kept)
    kx_c = swap(kx, "head", 1)
    kx_far = []
    for mask in masks:
        got = swap(kx, "head", mask)
        kx_far += [got, swap(got, "head", 1)]
    total = total_part([kx, kx_c], w_near)
    near_sums = []
    for c in range(GROUPS):
        near_sums.append(near_part(c, kept[c], tokens_c, w_near, p_near))
    w_far, p_far = fetch(
        (from_hbm(value_weight), 0, feat, far_at), (from_hbm(pair_weight), 0, feat, far_at)
    )
    pieces = tuple(width * p // sum(PARTS) for p in PARTS)
    sums = list(total_part(kx_far, w_far, total, pieces))

    far = []
    for bit in range(ctx_bits):
        mask = 1 << bit
        if bit == ctx_bits - 1:
            mask |= mask >> 1
        got = [swap(s, "ctx", mask) for s in sums]
        if bit < ctx_bits - 1:
            for g, value in enumerate(got):
                sums[g] = add_part(sums[g], value)
            far += got

    weight_c = swap(output_weight, "head", 1)

    queries, near, states = [], [], []
    for c in range(spans):
        group = c * GROUPS // spans
        vals, pair = near_sums[group]
        q, part, state = span_part(
            c, spans, far_x[group], w_far, p_far, vals, pair, mixing, states, pieces, far
        )
        queries.append(q)
        near.append(part)
        states.append(state)

    gain = out_gain.reshape(1, width)
    step = SPAN // FIRST
    chunks = [(0, k * step, step) for k in range(FIRST)]
    chunks += [(c, 0, SPAN) for c in range(1, spans)]
    hidden, hidden_c = [], []
    for chunk in chunks:
        hid = hidden_part(
            chunk, queries[chunk[0]], got, pieces, mixing, near[chunk[0]], gain, levels - 1
        )
        hidden.append(hid)
        hidden_c.append(swap(hid, "head", 1))
    arrived = []
    for mask in masks:
        (w_own,) = fetch((from_hbm(output_weight), 1, block, (mask,)))
        (w_other,) = fetch((weight_c, 1, block, (mask,)))
        for k in range(len(chunks)):
            part = out_part(hidden[k], hidden_c[k], w_own, w_other)
            arrived.append(swap(part, "head", mask))
    w_own, w_other = fetch((from_hbm(output_weight), 1, block, (0,)), (weight_c, 1, block, (0,)))
    own = own_part(hidden, hidden_c, w_own, w_other)
    n = len(chunks)
    early = [a for k, a in enumerate(arrived) if k % n < n - 1]
    out = sum_part(own, early, n - 1)
    return last_part(own, out, arrived[n - 1 :: n])


def solution(mesh):
    return jax.shard_map(
        local,
        mesh=mesh,
        in_specs=(
            P("ctx", "head"),
            P(),
            P(None, "head"),
            P("head", None),
            P("ctx", None),
            P(None, None, "head"),
            P("head"),
        ),
        out_specs=P("ctx", "head"),
        check_vma=False,
    )
```

```python
import functools
import math

import jax
import jax.numpy as jnp
from jax import lax
from jax.experimental import pallas as pl
from jax.experimental.pallas import tpu as pltpu
from jax.sharding import PartitionSpec as P


DH = 128
DK = 128
SPAN = 128
EPS = 1e-06
MIB = 1 << 20


F32 = jnp.float32
BF16 = jnp.bfloat16


def swap(value, axis, mask):
    pairs = [(s, s ^ mask) for s in range(lax.axis_size(axis))]
    return lax.ppermute(value, axis, pairs)


def from_hbm(value):
    return pltpu.with_memory_space_constraint(value, pltpu.HBM)


def from_vmem(value):
    return pltpu.with_memory_space_constraint(value, pltpu.VMEM)


def block_copies(picks, sources, targets, sems):
    head = lax.axis_index("head")
    copies = []
    for (axis, size, offsets), src, dst in zip(picks, sources, targets):
        for k, e in enumerate(offsets):
            start = pl.multiple_of((head ^ e) * size, size)
            view = src.at[pl.ds(start, size)] if axis == 0 else src.at[:, pl.ds(start, size)]
            rows = size if axis == 0 else src.shape[0]
            copies.append(
                pltpu.make_async_copy(view, dst.at[k * rows : (k + 1) * rows], sems.at[len(copies)])
            )
    return copies


def block_shapes(picks):
    shapes = []
    for a, axis, size, offsets in picks:
        shape = (size, a.shape[1]) if axis == 0 else (a.shape[0], size)
        shapes.append(pltpu.VMEM((shape[0] * len(offsets), shape[1]), a.dtype))
    return tuple(shapes)


def fetch_kernel(picks, *refs):
    n = len(picks)
    copies = block_copies(picks, refs[:n], refs[n:-1], refs[-1])
    for copy in copies:
        copy.start()
    for copy in copies:
        copy.wait()


def fetch(*picks):
    n = len(picks)
    copies = sum(len(p[3]) for p in picks)
    return pl.pallas_call(
        functools.partial(fetch_kernel, [p[1:] for p in picks]),
        out_shape=block_shapes(picks),
        in_specs=[pl.BlockSpec(memory_space=pl.ANY)] * n,
        out_specs=(pl.BlockSpec(memory_space=pltpu.VMEM),) * n,
        scratch_shapes=[pltpu.SemaphoreType.DMA((copies,))],
        compiler_params=params(1),
        cost_estimate=cost(0, 8 * MIB),
        name="fetch",
    )(*[p[0] for p in picks])


def unit_rows(values):
    scale = lax.rsqrt(jnp.mean(values * values, axis=-1, keepdims=True) + EPS)
    return values * scale / math.sqrt(values.shape[-1])


def mm(a, b):
    return jnp.dot(a, b, preferred_element_type=F32)


def mm_t(a, b):
    return lax.dot_general(a, b, (((0,), (0,)), ((), ())), preferred_element_type=F32)


def params(limit):
    return pltpu.CompilerParams(vmem_limit_bytes=limit * MIB)


def cost(flops, nbytes):
    return pl.CostEstimate(flops=flops, bytes_accessed=nbytes, transcendentals=0)


def full(shape):
    return pl.BlockSpec(shape, lambda *_: (0,) * len(shape))


def key_part_kernel(x_ref, w_ref, out_ref, *refs):
    kept, (w, sems) = refs[:-2], refs[-2:]
    feat = x_ref.shape[1]
    start = pl.multiple_of(lax.axis_index("head") * feat, feat)
    copies = [
        pltpu.make_async_copy(w_ref.at[pl.ds(start, feat), pl.ds(DK, DK)], w, sems.at[len(kept)])
    ]
    size = kept[0].shape[0]
    for c, ref in enumerate(kept):
        at = pl.ds(c * size, size)
        copies.append(pltpu.make_async_copy(x_ref.at[at], ref, sems.at[c]))
    for copy in copies:
        copy.start()
    copies[0].wait()
    for c, ref in enumerate(kept):
        copies[1 + c].wait()
        out_ref[c * size : (c + 1) * size] = mm(ref[...], w[...]).astype(BF16)


def key_part(tokens, pair_weight, chunks):
    rows, feat = tokens.shape
    return pl.pallas_call(
        key_part_kernel,
        out_shape=(jax.ShapeDtypeStruct((rows, DK), BF16),)
        + (pltpu.VMEM((rows // chunks, feat), BF16),) * chunks,
        in_specs=[pl.BlockSpec(memory_space=pltpu.HBM)] * 2,
        out_specs=(pl.BlockSpec(memory_space=pltpu.VMEM),) * (1 + chunks),
        scratch_shapes=[pltpu.VMEM((feat, DK), BF16), pltpu.SemaphoreType.DMA((1 + chunks,))],
        compiler_params=params(4),
        cost_estimate=cost(2 * rows * feat * DK, 2 * rows * feat),
        name="key_part",
    )(from_hbm(tokens), from_hbm(pair_weight))


def key_tokens_kernel(n, halves, *refs):
    part_refs, x_refs, out_refs = refs[:n], refs[n:-halves], refs[-halves:]
    total = part_refs[0][...].astype(F32)
    for ref in part_refs[1:]:
        total = total + ref[...].astype(F32)
    keys = unit_rows(total).astype(BF16)
    out = None
    size = x_refs[0].shape[0]
    for c, ref in enumerate(x_refs):
        part = mm_t(keys[c * size : (c + 1) * size], ref[...])
        out = part if out is None else out + part
    size = out_refs[0].shape[1]
    for p, ref in enumerate(out_refs):
        ref[...] = out[:, p * size : (p + 1) * size].astype(BF16)


def key_tokens(parts, kept, halves):
    feat = kept[0].shape[1]
    return pl.pallas_call(
        functools.partial(key_tokens_kernel, len(parts), halves),
        out_shape=(jax.ShapeDtypeStruct((DK, feat // halves), BF16),) * halves,
        compiler_params=params(4),
        cost_estimate=cost(2 * kept[0].size * len(kept) * DK, 2 * kept[0].size * len(kept)),
        name="key_tokens",
    )(*parts, *[from_vmem(k) for k in kept])


def mix_kernel(ctx_bits, index_ref, table_ref, out_ref, wide):
    levels, heads, size = table_ref.shape
    ctx = lax.axis_index("ctx")
    wide[...] = jnp.zeros_like(wide)
    hot = []
    for l in range(levels):
        table = table_ref[l]
        bit = l - (levels - ctx_bits)
        if bit >= 0:
            table = table * ((ctx >> bit) & 1).astype(F32)
        wide[l * heads : (l + 1) * heads, l * size : (l + 1) * size] = table
        ids = lax.broadcasted_iota(jnp.int32, (size, index_ref.shape[1]), 0)
        hot.append((ids == index_ref[l : l + 1, :]).astype(F32))
    hot = jnp.concatenate(hot, axis=0).astype(BF16)
    rest = wide[...]
    total = None
    for _ in range(3):
        part = rest.astype(BF16)
        rest = rest - part.astype(F32)
        value = lax.dot_general(hot, part, (((0,), (1,)), ((), ())), preferred_element_type=F32)
        total = value if total is None else total + value
    out_ref[...] = total


def mix_part(level_index, level_table, ctx_bits):
    rows = level_index.shape[0]
    levels, size, heads = level_table.shape
    return pl.pallas_call(
        functools.partial(mix_kernel, ctx_bits),
        out_shape=jax.ShapeDtypeStruct((rows, levels * heads), F32),
        scratch_shapes=[pltpu.VMEM((levels * heads, levels * size), F32)],
        compiler_params=params(4),
        cost_estimate=cost(6 * rows * levels * levels * heads * size, 4 * rows * levels * heads),
        name="mix_part",
    )(level_index.T, level_table.transpose(0, 2, 1))


def near_kernel(chunk, x0, x1, w_ref, p_ref, vals_ref, pair_ref):
    rows, feat = x0.shape
    a, b = x0[...], x1[chunk * rows : (chunk + 1) * rows]
    vals_ref[...] = mm(a, w_ref[:feat]) + mm(b, w_ref[feat:])
    pair_ref[...] = mm(a, p_ref[:feat]) + mm(b, p_ref[feat:])


def near_part(chunk, kept, tokens_c, weight, pair_weight):
    rows, feat = kept.shape
    width = weight.shape[1]
    return pl.pallas_call(
        functools.partial(near_kernel, chunk),
        out_shape=(
            jax.ShapeDtypeStruct((rows, width), F32),
            jax.ShapeDtypeStruct((rows, 2 * DK), F32),
        ),
        compiler_params=params(6),
        cost_estimate=cost(4 * rows * feat * width, 4 * feat * width),
        name="near_part",
    )(from_vmem(kept), tokens_c, from_vmem(weight), from_vmem(pair_weight))


def total_kernel(starts, has_acc, *refs):
    n = len(starts)
    w_ref = refs[n]
    total = refs[n + 1][...] if has_acc else None
    for ref, start in zip(refs, starts):
        part = mm(ref[...], w_ref[start : start + ref.shape[1]])
        total = part if total is None else total + part
    outs = refs[n + 1 + has_acc :]
    start = 0
    for ref in outs:
        stop = start + ref.shape[1]
        ref[...] = total[:, start:stop].astype(ref.dtype)
        start = stop


def total_part(lhs, starts, weight, acc=None, pieces=None):
    rows = lhs[0].shape[0]
    width = weight.shape[1]
    operands = [*lhs, from_vmem(weight)]
    if acc is not None:
        operands.append(acc)
    if pieces is None:
        out_shape = (jax.ShapeDtypeStruct((rows, width), F32),)
    else:
        out_shape = tuple(jax.ShapeDtypeStruct((rows, p), BF16) for p in pieces)
    size = sum(a.shape[1] for a in lhs)
    return pl.pallas_call(
        functools.partial(total_kernel, tuple(starts), acc is not None),
        out_shape=out_shape,
        compiler_params=params(8),
        cost_estimate=cost(2 * rows * size * width, 2 * size * width),
        name="total_part",
    )(*operands)


def add_kernel(a_ref, b_ref, out_ref):
    out_ref[...] = (a_ref[...].astype(F32) + b_ref[...].astype(F32)).astype(BF16)


def add_part(a, b):
    return pl.pallas_call(
        add_kernel,
        out_shape=jax.ShapeDtypeStruct(a.shape, BF16),
        compiler_params=params(2),
        cost_estimate=cost(a.size, 6 * a.size),
        name="add_part",
    )(a, b)


def head_places(pieces):
    return [(g, slice(k * DH, (k + 1) * DH)) for g, p in enumerate(pieces) for k in range(p // DH)]


def needed(span, bits):
    tops = [(span >> b << b, 1 << b) for b in range(bits) if span >> b & 1]
    return [list(range(top - size, top)) for top, size in tops]


def span_kernel(span, row, bits, n_far, keep, pieces, n_remote, *refs):
    far = refs[:n_far]
    w_ref, p_ref, v0_ref, p0_ref, mix_ref = refs[n_far : n_far + 5]
    buckets = needed(span, bits)
    first = min((j for js in buckets for j in js), default=span)
    states = {j: refs[n_far + 5 + j - first] for j in range(first, span)}
    remote = refs[n_far + 5 + span - first :]
    outs = remote[n_remote:]
    q_ref, out_ref = outs[0], outs[1]
    feat = far[0].shape[1]
    heads = out_ref.shape[1] // DH
    rows = slice(row, row + SPAN)
    vals, pair = v0_ref[rows], p0_ref[rows]
    for e in range(n_far):
        at = slice(e * feat, (e + 1) * feat)
        x = far[e][rows]
        vals = vals + mm(x, w_ref[at])
        pair = pair + mm(x, p_ref[at])
    queries = unit_rows(pair[:, :DK]).astype(BF16)
    keys = unit_rows(pair[:, DK:]).astype(BF16)
    vals = vals.astype(BF16)
    q_ref[...] = queries
    causal = (
        lax.broadcasted_iota(jnp.int32, (SPAN, SPAN), 0)
        >= lax.broadcasted_iota(jnp.int32, (SPAN, SPAN), 1)
    )
    scores = lax.dot_general(queries, keys, (((1,), (1,)), ((), ())), preferred_element_type=F32)
    scores = jnp.where(causal, scores, 0.0).astype(BF16)
    reads = [(0, mm(scores, vals))]
    levels = [1 + b for b in range(bits) if span >> b & 1]
    for level, js in zip(levels, buckets):
        bucket = states[js[0]][...]
        for j in js[1:]:
            bucket = bucket + states[j][...]
        reads.append((level, mm(queries, bucket.astype(BF16))))
    if keep:
        outs[2][...] = mm_t(keys, vals)
    places = head_places(pieces)
    for h in range(heads):
        cols = slice(h * DH, (h + 1) * DH)
        total = None
        for level, value in reads:
            col = level * heads + h
            part = value[:, cols] * mix_ref[:, col : col + 1]
            total = part if total is None else total + part
        g, at = places[h]
        for b in range(n_remote // len(pieces)):
            col = (1 + bits + b) * heads + h
            value = mm(queries, remote[b * len(pieces) + g][:, at])
            total = total + value * mix_ref[:, col : col + 1]
        out_ref[:, cols] = total


def span_part(span, spans, far, weight, pair_weight, vals, pair, mixing, states, pieces, remote):
    feat = far[0].shape[1]
    width = weight.shape[1]
    bits = spans.bit_length() - 1
    n_far = len(far)
    first = min((j for js in needed(span, bits) for j in js), default=span)
    prior = states[first:span]
    keep = span < spans - 1
    row = span * SPAN % far[0].shape[0]

    def whole(value):
        return pl.BlockSpec(value.shape, lambda i: (0, 0))

    out_shape = [
        jax.ShapeDtypeStruct((SPAN, DK), BF16),
        jax.ShapeDtypeStruct((SPAN, width), F32),
    ]
    if keep:
        out_shape.append(jax.ShapeDtypeStruct((DK, width), F32))
    vmem = pl.BlockSpec(memory_space=pltpu.VMEM)
    out = pl.pallas_call(
        functools.partial(span_kernel, span, row, bits, n_far, keep, pieces, len(remote)),
        out_shape=out_shape,
        grid=(1,),
        in_specs=[vmem] * (n_far + 4)
        + [pl.BlockSpec((SPAN, mixing.shape[1]), lambda i: (span, 0))]
        + [whole(p) for p in [*prior, *remote]],
        out_specs=[whole(o) for o in out_shape],
        compiler_params=params(6),
        cost_estimate=cost(2 * SPAN * feat * width * n_far, 2 * n_far * feat * width),
        name="span_part",
    )(*far, from_vmem(weight), from_vmem(pair_weight), vals, pair, mixing, *prior, *remote)
    return out[0], out[1], (out[2] if keep else None)


def hidden_kernel(pieces, level, q_ref, *refs):
    last = refs[: len(pieces)]
    mix_ref, near_ref, gain_ref, out_ref = refs[len(pieces) :]
    heads = out_ref.shape[1] // DH
    for h, (g, at) in enumerate(head_places(pieces)):
        cols = slice(h * DH, (h + 1) * DH)
        col = level * heads + h
        value = mm(q_ref[...], last[g][:, at])
        total = near_ref[:, cols] + value * mix_ref[:, col : col + 1]
        scale = lax.rsqrt(jnp.mean(total * total, axis=-1, keepdims=True) + EPS)
        out_ref[:, cols] = (total * scale * gain_ref[:, cols]).astype(BF16)


def hidden_part(chunk, queries, last, pieces, mixing, near, gain, level):
    span, start, size = chunk
    width = near.shape[1]

    def rows(cols):
        return pl.BlockSpec((size, cols), lambda k: (start // size, 0))

    return pl.pallas_call(
        functools.partial(hidden_kernel, pieces, level),
        out_shape=jax.ShapeDtypeStruct((size, width), BF16),
        grid=(1,),
        in_specs=[rows(DK)]
        + [full(f.shape) for f in last]
        + [
            pl.BlockSpec((size, mixing.shape[1]), lambda k: ((span * SPAN + start) // size, 0)),
            rows(width),
            full((1, width)),
        ],
        out_specs=full((size, width)),
        compiler_params=params(4),
        cost_estimate=cost(2 * size * DK * width, 6 * size * width),
        name="hidden_part",
    )(queries, *last, mixing, near, gain)


def out_kernel(*refs):
    out = refs[-1]
    total = refs[2][...] if len(refs) == 4 else None
    value = mm(refs[0][...], refs[1][...])
    out[...] = (value if total is None else total + value).astype(out.dtype)


def out_part(own, other, weight, weight_other):
    size, width = own.shape
    block = weight.shape[1]

    def part(a, w, acc, dtype):
        return pl.pallas_call(
            out_kernel,
            out_shape=jax.ShapeDtypeStruct((size, block), dtype),
            compiler_params=params(8),
            cost_estimate=cost(2 * size * width * block, 2 * width * block),
            name="out_part",
        )(a, from_vmem(w), *acc)

    acc = part(own, weight, (), F32)
    return part(other, weight_other, (acc,), BF16)


def own_kernel(chunks, *refs):
    own, other = refs[:chunks], refs[chunks : 2 * chunks]
    w_ref, v_ref, out_ref, xa, xb = refs[2 * chunks :]
    start = 0
    for a, b in zip(own, other):
        stop = start + a.shape[0]
        xa[start:stop] = a[...]
        xb[start:stop] = b[...]
        start = stop
    out_ref[...] = mm(xa[...], w_ref[...]) + mm(xb[...], v_ref[...])


def own_part(own, other, weight, weight_other):
    rows = sum(a.shape[0] for a in own)
    width = own[0].shape[1]
    block = weight.shape[1]
    return pl.pallas_call(
        functools.partial(own_kernel, len(own)),
        out_shape=jax.ShapeDtypeStruct((rows, block), F32),
        scratch_shapes=[pltpu.VMEM((rows, width), BF16)] * 2,
        compiler_params=params(6),
        cost_estimate=cost(4 * rows * width * block, 4 * width * block),
        name="own_part",
    )(*own, *other, from_vmem(weight), from_vmem(weight_other))


def sum_kernel(chunks, acc_ref, *refs):
    arrived, out_ref, stage, sem = refs[:-3], refs[-3], refs[-2], refs[-1]
    start = 0
    for c in range(chunks):
        stop = start + arrived[c].shape[0]
        total = acc_ref[start:stop]
        for ref in arrived[c::chunks]:
            total = total + ref[...].astype(F32)
        stage[start:stop] = total.astype(BF16)
        start = stop
    copy = pltpu.make_async_copy(stage, out_ref.at[0:start], sem)
    copy.start()
    copy.wait()


def sum_part(acc, arrived, chunks):
    rows = sum(a.shape[0] for a in arrived[:chunks])
    vmem = pl.BlockSpec(memory_space=pltpu.VMEM)
    return pl.pallas_call(
        functools.partial(sum_kernel, chunks),
        out_shape=jax.ShapeDtypeStruct(acc.shape, BF16),
        in_specs=[vmem] * (1 + len(arrived)),
        out_specs=pl.BlockSpec(memory_space=pl.ANY),
        scratch_shapes=[pltpu.VMEM((rows, acc.shape[1]), BF16), pltpu.SemaphoreType.DMA(())],
        compiler_params=params(4),
        cost_estimate=cost(acc.size, 8 * acc.size),
        name="sum_part",
    )(acc, *arrived)


def last_kernel(n, acc_ref, done_ref, *refs):
    arrived, (out_ref, stage, sem) = refs[:n], refs[n:]
    rows = stage.shape[0]
    total = acc_ref[-rows:]
    for ref in arrived:
        total = total + ref[...].astype(F32)
    stage[...] = total.astype(BF16)
    copy = pltpu.make_async_copy(stage, out_ref.at[out_ref.shape[0] - rows :], sem)
    copy.start()
    copy.wait()


def last_part(acc, done, arrived):
    rows = arrived[0].shape[0]
    vmem = pl.BlockSpec(memory_space=pltpu.VMEM)
    hbm = pl.BlockSpec(memory_space=pl.ANY)
    return pl.pallas_call(
        functools.partial(last_kernel, len(arrived)),
        out_shape=jax.ShapeDtypeStruct(acc.shape, BF16),
        in_specs=[vmem, hbm] + [vmem] * len(arrived),
        out_specs=hbm,
        input_output_aliases={1: 0},
        scratch_shapes=[pltpu.VMEM((rows, acc.shape[1]), BF16), pltpu.SemaphoreType.DMA(())],
        compiler_params=params(2),
        cost_estimate=cost(acc.size, 2 * acc.size),
        name="last_part",
    )(acc, done, *arrived)


PARTS = (3, 5)
GROUPS = 2
HALVES = 2
FIRST = 1


def local(tokens, pair_weight, value_weight, output_weight, level_index, level_table, out_gain):
    rows = tokens.shape[0]
    width = value_weight.shape[1]
    n_head = lax.axis_size("head")
    n_ctx = lax.axis_size("ctx")
    ctx_bits = n_ctx.bit_length() - 1
    levels = level_table.shape[0]
    spans = rows // SPAN
    block = output_weight.shape[1] // n_head
    masks = range(2, n_head, 2)

    feat = tokens.shape[1]
    near_at, far_at = (0, 1), tuple(range(2, n_head))

    own_key, *kept = key_part(tokens, pair_weight, GROUPS)
    parts = [own_key, swap(own_key, "head", 1)]
    for mask in masks:
        got = swap(own_key, "head", mask)
        parts += [got, swap(got, "head", 1)]

    mixing = mix_part(level_index, level_table, ctx_bits)

    tokens_c = swap(tokens, "head", 1)
    far_x = []
    for c in range(GROUPS):
        far = []
        for mask in masks:
            got = swap(kept[c], "head", mask)
            far += [got, swap(got, "head", 1)]
        far_x.append(far)

    w_near, *w_outs = fetch(
        (from_hbm(value_weight), 0, feat, near_at),
        *((from_hbm(output_weight), 1, block, (mask,)) for mask in masks),
    )
    kx = key_tokens(parts, kept, HALVES)
    half = feat // HALVES
    kx_near = [*kx, *(swap(k, "head", 1) for k in kx)]
    kx_far = []
    for k in kx:
        far = []
        for mask in masks:
            got = swap(k, "head", mask)
            far += [got, swap(got, "head", 1)]
        kx_far.append(far)
    (total,) = total_part(kx_near, range(0, 2 * feat, half), w_near)
    w_far, p_far, p_near = fetch(
        (from_hbm(value_weight), 0, feat, far_at),
        (from_hbm(pair_weight), 0, feat, far_at),
        (from_hbm(pair_weight), 0, feat, near_at),
    )
    near_sums = []
    for c in range(GROUPS):
        near_sums.append(near_part(c, kept[c], tokens_c, w_near, p_near))
    pieces = tuple(width * p // sum(PARTS) for p in PARTS)
    for p, far in enumerate(kx_far):
        starts = range(p * half, len(far) * feat, feat)
        out = total_part(far, starts, w_far, total, pieces if p == HALVES - 1 else None)
        total = out[0]
    sums = list(out)

    far = []
    for bit in range(ctx_bits):
        mask = 1 << bit
        if bit == ctx_bits - 1:
            mask |= mask >> 1
        got = [swap(s, "ctx", mask) for s in sums]
        if bit < ctx_bits - 1:
            for g, value in enumerate(got):
                sums[g] = add_part(sums[g], value)
            far += got

    weight_c = swap(output_weight, "head", 1)

    queries, near, states = [], [], []
    for c in range(spans):
        group = c * GROUPS // spans
        vals, pair = near_sums[group]
        q, part, state = span_part(
            c, spans, far_x[group], w_far, p_far, vals, pair, mixing, states, pieces, far
        )
        queries.append(q)
        near.append(part)
        states.append(state)

    gain = out_gain.reshape(1, width)
    step = SPAN // FIRST
    chunks = [(0, k * step, step) for k in range(FIRST)]
    chunks += [(c, 0, SPAN) for c in range(1, spans)]
    hidden, hidden_c = [], []
    for chunk in chunks:
        hid = hidden_part(
            chunk, queries[chunk[0]], got, pieces, mixing, near[chunk[0]], gain, levels - 1
        )
        hidden.append(hid)
        hidden_c.append(swap(hid, "head", 1))
    arrived = []
    for mask, w_own in zip(masks, w_outs):
        (w_other,) = fetch((weight_c, 1, block, (mask,)))
        for k in range(len(chunks)):
            part = out_part(hidden[k], hidden_c[k], w_own, w_other)
            arrived.append(swap(part, "head", mask))
    w_own, w_other = fetch((from_hbm(output_weight), 1, block, (0,)), (weight_c, 1, block, (0,)))
    own = own_part(hidden, hidden_c, w_own, w_other)
    n = len(chunks)
    early = [a for k, a in enumerate(arrived) if k % n < n - 1]
    out = sum_part(own, early, n - 1)
    return last_part(own, out, arrived[n - 1 :: n])


def solution(mesh):
    return jax.shard_map(
        local,
        mesh=mesh,
        in_specs=(
            P("ctx", "head"),
            P(),
            P(None, "head"),
            P("head", None),
            P("ctx", None),
            P(None, None, "head"),
            P("head"),
        ),
        out_specs=P("ctx", "head"),
        check_vma=False,
    )
```

```python
import functools
import math

import jax
import jax.numpy as jnp
from jax import lax
from jax.experimental import pallas as pl
from jax.experimental.pallas import tpu as pltpu
from jax.sharding import PartitionSpec as P


DH = 128
DK = 128
SPAN = 128
EPS = 1e-06
MIB = 1 << 20


F32 = jnp.float32
BF16 = jnp.bfloat16


def swap(value, axis, mask):
    pairs = [(s, s ^ mask) for s in range(lax.axis_size(axis))]
    return lax.ppermute(value, axis, pairs)


def from_hbm(value):
    return pltpu.with_memory_space_constraint(value, pltpu.HBM)


def from_vmem(value):
    return pltpu.with_memory_space_constraint(value, pltpu.VMEM)


def block_copies(picks, sources, targets, sems):
    head = lax.axis_index("head")
    copies = []
    for (axis, size, offsets), src, dst in zip(picks, sources, targets):
        for k, e in enumerate(offsets):
            start = pl.multiple_of((head ^ e) * size, size)
            view = src.at[pl.ds(start, size)] if axis == 0 else src.at[:, pl.ds(start, size)]
            rows = size if axis == 0 else src.shape[0]
            copies.append(
                pltpu.make_async_copy(view, dst.at[k * rows : (k + 1) * rows], sems.at[len(copies)])
            )
    return copies


def block_shapes(picks):
    shapes = []
    for a, axis, size, offsets in picks:
        shape = (size, a.shape[1]) if axis == 0 else (a.shape[0], size)
        shapes.append(pltpu.VMEM((shape[0] * len(offsets), shape[1]), a.dtype))
    return tuple(shapes)


def fetch_kernel(picks, *refs):
    n = len(picks)
    copies = block_copies(picks, refs[:n], refs[n:-1], refs[-1])
    for copy in copies:
        copy.start()
    for copy in copies:
        copy.wait()


def fetch(*picks):
    n = len(picks)
    copies = sum(len(p[3]) for p in picks)
    return pl.pallas_call(
        functools.partial(fetch_kernel, [p[1:] for p in picks]),
        out_shape=block_shapes(picks),
        in_specs=[pl.BlockSpec(memory_space=pl.ANY)] * n,
        out_specs=(pl.BlockSpec(memory_space=pltpu.VMEM),) * n,
        scratch_shapes=[pltpu.SemaphoreType.DMA((copies,))],
        compiler_params=params(1),
        cost_estimate=cost(0, 8 * MIB),
    )(*[p[0] for p in picks])


def unit_rows(values):
    scale = lax.rsqrt(jnp.mean(values * values, axis=-1, keepdims=True) + EPS)
    return values * scale / math.sqrt(values.shape[-1])


def mm(a, b):
    return jnp.dot(a, b, preferred_element_type=F32)


def mm_t(a, b):
    return lax.dot_general(a, b, (((0,), (0,)), ((), ())), preferred_element_type=F32)


def params(limit):
    return pltpu.CompilerParams(vmem_limit_bytes=limit * MIB)


def cost(flops, nbytes):
    return pl.CostEstimate(flops=flops, bytes_accessed=nbytes, transcendentals=0)


def full(shape):
    return pl.BlockSpec(shape, lambda *_: (0,) * len(shape))


def key_part_kernel(x_ref, w_ref, out_ref, *refs):
    kept, (w, sems) = refs[:-2], refs[-2:]
    feat = x_ref.shape[1]
    start = pl.multiple_of(lax.axis_index("head") * feat, feat)
    copies = [
        pltpu.make_async_copy(w_ref.at[pl.ds(start, feat), pl.ds(DK, DK)], w, sems.at[len(kept)])
    ]
    size = kept[0].shape[0]
    for c, ref in enumerate(kept):
        at = pl.ds(c * size, size)
        copies.append(pltpu.make_async_copy(x_ref.at[at], ref, sems.at[c]))
    for copy in copies:
        copy.start()
    copies[0].wait()
    for c, ref in enumerate(kept):
        copies[1 + c].wait()
        out_ref[c * size : (c + 1) * size] = mm(ref[...], w[...]).astype(BF16)


def key_part(tokens, pair_weight, chunks):
    rows, feat = tokens.shape
    return pl.pallas_call(
        key_part_kernel,
        out_shape=(jax.ShapeDtypeStruct((rows, DK), BF16),)
        + (pltpu.VMEM((rows // chunks, feat), BF16),) * chunks,
        in_specs=[pl.BlockSpec(memory_space=pltpu.HBM)] * 2,
        out_specs=(pl.BlockSpec(memory_space=pltpu.VMEM),) * (1 + chunks),
        scratch_shapes=[pltpu.VMEM((feat, DK), BF16), pltpu.SemaphoreType.DMA((1 + chunks,))],
        compiler_params=params(4),
        cost_estimate=cost(2 * rows * feat * DK, 2 * rows * feat),
    )(from_hbm(tokens), from_hbm(pair_weight))


def key_tokens_kernel(n, halves, *refs):
    part_refs, x_refs, out_refs = refs[:n], refs[n:-halves], refs[-halves:]
    total = part_refs[0][...].astype(F32)
    for ref in part_refs[1:]:
        total = total + ref[...].astype(F32)
    keys = unit_rows(total).astype(BF16)
    out = None
    size = x_refs[0].shape[0]
    for c, ref in enumerate(x_refs):
        part = mm_t(keys[c * size : (c + 1) * size], ref[...])
        out = part if out is None else out + part
    size = out_refs[0].shape[1]
    for p, ref in enumerate(out_refs):
        ref[...] = out[:, p * size : (p + 1) * size].astype(BF16)


def key_tokens(parts, kept, halves):
    feat = kept[0].shape[1]
    return pl.pallas_call(
        functools.partial(key_tokens_kernel, len(parts), halves),
        out_shape=(jax.ShapeDtypeStruct((DK, feat // halves), BF16),) * halves,
        compiler_params=params(4),
        cost_estimate=cost(2 * kept[0].size * len(kept) * DK, 2 * kept[0].size * len(kept)),
    )(*parts, *[from_vmem(k) for k in kept])


def mix_kernel(ctx_bits, index_ref, table_ref, out_ref, wide):
    levels, heads, size = table_ref.shape
    ctx = lax.axis_index("ctx")
    wide[...] = jnp.zeros_like(wide)
    hot = []
    for l in range(levels):
        table = table_ref[l]
        bit = l - (levels - ctx_bits)
        if bit >= 0:
            table = table * ((ctx >> bit) & 1).astype(F32)
        wide[l * heads : (l + 1) * heads, l * size : (l + 1) * size] = table
        ids = lax.broadcasted_iota(jnp.int32, (size, index_ref.shape[1]), 0)
        hot.append((ids == index_ref[l : l + 1, :]).astype(F32))
    hot = jnp.concatenate(hot, axis=0).astype(BF16)
    rest = wide[...]
    total = None
    for _ in range(3):
        part = rest.astype(BF16)
        rest = rest - part.astype(F32)
        value = lax.dot_general(hot, part, (((0,), (1,)), ((), ())), preferred_element_type=F32)
        total = value if total is None else total + value
    out_ref[...] = total


def mix_part(level_index, level_table, ctx_bits):
    rows = level_index.shape[0]
    levels, size, heads = level_table.shape
    return pl.pallas_call(
        functools.partial(mix_kernel, ctx_bits),
        out_shape=jax.ShapeDtypeStruct((rows, levels * heads), F32),
        scratch_shapes=[pltpu.VMEM((levels * heads, levels * size), F32)],
        compiler_params=params(4),
        cost_estimate=cost(6 * rows * levels * levels * heads * size, 4 * rows * levels * heads),
    )(level_index.T, level_table.transpose(0, 2, 1))


def near_kernel(chunk, x0, x1, w_ref, p_ref, vals_ref, pair_ref):
    rows, feat = x0.shape
    a, b = x0[...], x1[chunk * rows : (chunk + 1) * rows]
    vals_ref[...] = mm(a, w_ref[:feat]) + mm(b, w_ref[feat:])
    pair_ref[...] = mm(a, p_ref[:feat]) + mm(b, p_ref[feat:])


def near_part(chunk, kept, tokens_c, weight, pair_weight):
    rows, feat = kept.shape
    width = weight.shape[1]
    return pl.pallas_call(
        functools.partial(near_kernel, chunk),
        out_shape=(
            jax.ShapeDtypeStruct((rows, width), F32),
            jax.ShapeDtypeStruct((rows, 2 * DK), F32),
        ),
        compiler_params=params(6),
        cost_estimate=cost(4 * rows * feat * width, 4 * feat * width),
    )(from_vmem(kept), tokens_c, from_vmem(weight), from_vmem(pair_weight))


def total_kernel(starts, has_acc, *refs):
    n = len(starts)
    w_ref = refs[n]
    total = refs[n + 1][...] if has_acc else None
    for ref, start in zip(refs, starts):
        part = mm(ref[...], w_ref[start : start + ref.shape[1]])
        total = part if total is None else total + part
    outs = refs[n + 1 + has_acc :]
    start = 0
    for ref in outs:
        stop = start + ref.shape[1]
        ref[...] = total[:, start:stop].astype(ref.dtype)
        start = stop


def total_part(lhs, starts, weight, acc=None, pieces=None):
    rows = lhs[0].shape[0]
    width = weight.shape[1]
    operands = [*lhs, from_vmem(weight)]
    if acc is not None:
        operands.append(acc)
    if pieces is None:
        out_shape = (jax.ShapeDtypeStruct((rows, width), F32),)
    else:
        out_shape = tuple(jax.ShapeDtypeStruct((rows, p), BF16) for p in pieces)
    size = sum(a.shape[1] for a in lhs)
    return pl.pallas_call(
        functools.partial(total_kernel, tuple(starts), acc is not None),
        out_shape=out_shape,
        compiler_params=params(8),
        cost_estimate=cost(2 * rows * size * width, 2 * size * width),
    )(*operands)


def add_kernel(a_ref, b_ref, out_ref):
    out_ref[...] = (a_ref[...].astype(F32) + b_ref[...].astype(F32)).astype(BF16)


def add_part(a, b):
    return pl.pallas_call(
        add_kernel,
        out_shape=jax.ShapeDtypeStruct(a.shape, BF16),
        compiler_params=params(2),
        cost_estimate=cost(a.size, 6 * a.size),
    )(a, b)


def head_places(pieces):
    return [(g, slice(k * DH, (k + 1) * DH)) for g, p in enumerate(pieces) for k in range(p // DH)]


def needed(span, bits):
    tops = [(span >> b << b, 1 << b) for b in range(bits) if span >> b & 1]
    return [list(range(top - size, top)) for top, size in tops]


def span_kernel(span, row, bits, n_far, keep, pieces, n_remote, *refs):
    far = refs[:n_far]
    w_ref, p_ref, v0_ref, p0_ref, mix_ref = refs[n_far : n_far + 5]
    buckets = needed(span, bits)
    first = min((j for js in buckets for j in js), default=span)
    states = {j: refs[n_far + 5 + j - first] for j in range(first, span)}
    remote = refs[n_far + 5 + span - first :]
    outs = remote[n_remote:]
    q_ref, out_ref = outs[0], outs[1]
    feat = far[0].shape[1]
    heads = out_ref.shape[1] // DH
    rows = slice(row, row + SPAN)
    vals, pair = v0_ref[rows], p0_ref[rows]
    for e in range(n_far):
        at = slice(e * feat, (e + 1) * feat)
        x = far[e][rows]
        vals = vals + mm(x, w_ref[at])
        pair = pair + mm(x, p_ref[at])
    queries = unit_rows(pair[:, :DK]).astype(BF16)
    keys = unit_rows(pair[:, DK:]).astype(BF16)
    vals = vals.astype(BF16)
    q_ref[...] = queries
    causal = (
        lax.broadcasted_iota(jnp.int32, (SPAN, SPAN), 0)
        >= lax.broadcasted_iota(jnp.int32, (SPAN, SPAN), 1)
    )
    scores = lax.dot_general(queries, keys, (((1,), (1,)), ((), ())), preferred_element_type=F32)
    scores = jnp.where(causal, scores, 0.0).astype(BF16)
    reads = [(0, mm(scores, vals))]
    levels = [1 + b for b in range(bits) if span >> b & 1]
    for level, js in zip(levels, buckets):
        bucket = states[js[0]][...]
        for j in js[1:]:
            bucket = bucket + states[j][...]
        reads.append((level, mm(queries, bucket.astype(BF16))))
    if keep:
        outs[2][...] = mm_t(keys, vals)
    places = head_places(pieces)
    for h in range(heads):
        cols = slice(h * DH, (h + 1) * DH)
        total = None
        for level, value in reads:
            col = level * heads + h
            part = value[:, cols] * mix_ref[:, col : col + 1]
            total = part if total is None else total + part
        g, at = places[h]
        for b in range(n_remote // len(pieces)):
            col = (1 + bits + b) * heads + h
            value = mm(queries, remote[b * len(pieces) + g][:, at])
            total = total + value * mix_ref[:, col : col + 1]
        out_ref[:, cols] = total


def span_part(span, spans, far, weight, pair_weight, vals, pair, mixing, states, pieces, remote):
    feat = far[0].shape[1]
    width = weight.shape[1]
    bits = spans.bit_length() - 1
    n_far = len(far)
    first = min((j for js in needed(span, bits) for j in js), default=span)
    prior = states[first:span]
    keep = span < spans - 1
    row = span * SPAN % far[0].shape[0]

    def whole(value):
        return pl.BlockSpec(value.shape, lambda i: (0, 0))

    out_shape = [
        jax.ShapeDtypeStruct((SPAN, DK), BF16),
        jax.ShapeDtypeStruct((SPAN, width), F32),
    ]
    if keep:
        out_shape.append(jax.ShapeDtypeStruct((DK, width), F32))
    vmem = pl.BlockSpec(memory_space=pltpu.VMEM)
    out = pl.pallas_call(
        functools.partial(span_kernel, span, row, bits, n_far, keep, pieces, len(remote)),
        out_shape=out_shape,
        grid=(1,),
        in_specs=[vmem] * (n_far + 4)
        + [pl.BlockSpec((SPAN, mixing.shape[1]), lambda i: (span, 0))]
        + [whole(p) for p in [*prior, *remote]],
        out_specs=[whole(o) for o in out_shape],
        compiler_params=params(6),
        cost_estimate=cost(2 * SPAN * feat * width * n_far, 2 * n_far * feat * width),
    )(*far, from_vmem(weight), from_vmem(pair_weight), vals, pair, mixing, *prior, *remote)
    return out[0], out[1], (out[2] if keep else None)


def hidden_kernel(pieces, level, q_ref, *refs):
    last = refs[: len(pieces)]
    mix_ref, near_ref, gain_ref, out_ref = refs[len(pieces) :]
    heads = out_ref.shape[1] // DH
    for h, (g, at) in enumerate(head_places(pieces)):
        cols = slice(h * DH, (h + 1) * DH)
        col = level * heads + h
        value = mm(q_ref[...], last[g][:, at])
        total = near_ref[:, cols] + value * mix_ref[:, col : col + 1]
        scale = lax.rsqrt(jnp.mean(total * total, axis=-1, keepdims=True) + EPS)
        out_ref[:, cols] = (total * scale * gain_ref[:, cols]).astype(BF16)


def hidden_part(chunk, queries, last, pieces, mixing, near, gain, level):
    span, start, size = chunk
    width = near.shape[1]

    def rows(cols):
        return pl.BlockSpec((size, cols), lambda k: (start // size, 0))

    return pl.pallas_call(
        functools.partial(hidden_kernel, pieces, level),
        out_shape=jax.ShapeDtypeStruct((size, width), BF16),
        grid=(1,),
        in_specs=[rows(DK)]
        + [full(f.shape) for f in last]
        + [
            pl.BlockSpec((size, mixing.shape[1]), lambda k: ((span * SPAN + start) // size, 0)),
            rows(width),
            full((1, width)),
        ],
        out_specs=full((size, width)),
        compiler_params=params(4),
        cost_estimate=cost(2 * size * DK * width, 6 * size * width),
    )(queries, *last, mixing, near, gain)


def out_kernel(*refs):
    out = refs[-1]
    total = refs[2][...] if len(refs) == 4 else None
    value = mm(refs[0][...], refs[1][...])
    out[...] = (value if total is None else total + value).astype(out.dtype)


def out_part(own, other, weight, weight_other):
    size, width = own.shape
    block = weight.shape[1]

    def part(a, w, acc, dtype):
        return pl.pallas_call(
            out_kernel,
            out_shape=jax.ShapeDtypeStruct((size, block), dtype),
            compiler_params=params(8),
            cost_estimate=cost(2 * size * width * block, 2 * width * block),
        )(a, from_vmem(w), *acc)

    acc = part(own, weight, (), F32)
    return part(other, weight_other, (acc,), BF16)


def own_kernel(chunks, *refs):
    own, other = refs[:chunks], refs[chunks : 2 * chunks]
    w_ref, v_ref, out_ref, xa, xb = refs[2 * chunks :]
    start = 0
    for a, b in zip(own, other):
        stop = start + a.shape[0]
        xa[start:stop] = a[...]
        xb[start:stop] = b[...]
        start = stop
    out_ref[...] = mm(xa[...], w_ref[...]) + mm(xb[...], v_ref[...])


def own_part(own, other, weight, weight_other):
    rows = sum(a.shape[0] for a in own)
    width = own[0].shape[1]
    block = weight.shape[1]
    return pl.pallas_call(
        functools.partial(own_kernel, len(own)),
        out_shape=jax.ShapeDtypeStruct((rows, block), F32),
        scratch_shapes=[pltpu.VMEM((rows, width), BF16)] * 2,
        compiler_params=params(6),
        cost_estimate=cost(4 * rows * width * block, 4 * width * block),
    )(*own, *other, from_vmem(weight), from_vmem(weight_other))


def sum_kernel(chunks, acc_ref, *refs):
    arrived, out_ref, stage, sem = refs[:-3], refs[-3], refs[-2], refs[-1]
    start = 0
    for c in range(chunks):
        stop = start + arrived[c].shape[0]
        total = acc_ref[start:stop]
        for ref in arrived[c::chunks]:
            total = total + ref[...].astype(F32)
        stage[start:stop] = total.astype(BF16)
        start = stop
    copy = pltpu.make_async_copy(stage, out_ref.at[0:start], sem)
    copy.start()
    copy.wait()


def sum_part(acc, arrived, chunks):
    rows = sum(a.shape[0] for a in arrived[:chunks])
    vmem = pl.BlockSpec(memory_space=pltpu.VMEM)
    return pl.pallas_call(
        functools.partial(sum_kernel, chunks),
        out_shape=jax.ShapeDtypeStruct(acc.shape, BF16),
        in_specs=[vmem] * (1 + len(arrived)),
        out_specs=pl.BlockSpec(memory_space=pl.ANY),
        scratch_shapes=[pltpu.VMEM((rows, acc.shape[1]), BF16), pltpu.SemaphoreType.DMA(())],
        compiler_params=params(4),
        cost_estimate=cost(acc.size, 8 * acc.size),
    )(acc, *arrived)


def last_kernel(n, acc_ref, done_ref, *refs):
    arrived, (out_ref, stage, sem) = refs[:n], refs[n:]
    rows = stage.shape[0]
    total = acc_ref[-rows:]
    for ref in arrived:
        total = total + ref[...].astype(F32)
    stage[...] = total.astype(BF16)
    copy = pltpu.make_async_copy(stage, out_ref.at[out_ref.shape[0] - rows :], sem)
    copy.start()
    copy.wait()


def last_part(acc, done, arrived):
    rows = arrived[0].shape[0]
    vmem = pl.BlockSpec(memory_space=pltpu.VMEM)
    hbm = pl.BlockSpec(memory_space=pl.ANY)
    return pl.pallas_call(
        functools.partial(last_kernel, len(arrived)),
        out_shape=jax.ShapeDtypeStruct(acc.shape, BF16),
        in_specs=[vmem, hbm] + [vmem] * len(arrived),
        out_specs=hbm,
        input_output_aliases={1: 0},
        scratch_shapes=[pltpu.VMEM((rows, acc.shape[1]), BF16), pltpu.SemaphoreType.DMA(())],
        compiler_params=params(2),
        cost_estimate=cost(acc.size, 2 * acc.size),
    )(acc, done, *arrived)


PARTS = (3, 5)
GROUPS = 2
HALVES = 2
FIRST = 1


def local(tokens, pair_weight, value_weight, output_weight, level_index, level_table, out_gain):
    rows = tokens.shape[0]
    width = value_weight.shape[1]
    n_head = lax.axis_size("head")
    n_ctx = lax.axis_size("ctx")
    ctx_bits = n_ctx.bit_length() - 1
    levels = level_table.shape[0]
    spans = rows // SPAN
    block = output_weight.shape[1] // n_head
    masks = range(2, n_head, 2)

    feat = tokens.shape[1]
    near_at, far_at = (0, 1), tuple(range(2, n_head))

    own_key, *kept = key_part(tokens, pair_weight, GROUPS)
    parts = [own_key, swap(own_key, "head", 1)]
    for mask in masks:
        got = swap(own_key, "head", mask)
        parts += [got, swap(got, "head", 1)]

    mixing = mix_part(level_index, level_table, ctx_bits)

    tokens_c = swap(tokens, "head", 1)
    far_x = []
    for c in range(GROUPS):
        far = []
        for mask in masks:
            got = swap(kept[c], "head", mask)
            far += [got, swap(got, "head", 1)]
        far_x.append(far)

    w_near, *w_outs = fetch(
        (from_hbm(value_weight), 0, feat, near_at),
        *((from_hbm(output_weight), 1, block, (mask,)) for mask in masks),
    )
    kx = key_tokens(parts, kept, HALVES)
    half = feat // HALVES
    kx_near = [*kx, *(swap(k, "head", 1) for k in kx)]
    kx_far = []
    for k in kx:
        far = []
        for mask in masks:
            got = swap(k, "head", mask)
            far += [got, swap(got, "head", 1)]
        kx_far.append(far)
    (total,) = total_part(kx_near, range(0, 2 * feat, half), w_near)
    w_far, p_far, p_near = fetch(
        (from_hbm(value_weight), 0, feat, far_at),
        (from_hbm(pair_weight), 0, feat, far_at),
        (from_hbm(pair_weight), 0, feat, near_at),
    )
    near_sums = []
    for c in range(GROUPS):
        near_sums.append(near_part(c, kept[c], tokens_c, w_near, p_near))
    pieces = tuple(width * p // sum(PARTS) for p in PARTS)
    for p, far in enumerate(kx_far):
        starts = range(p * half, len(far) * feat, feat)
        out = total_part(far, starts, w_far, total, pieces if p == HALVES - 1 else None)
        total = out[0]
    sums = list(out)

    far = []
    for bit in range(ctx_bits):
        mask = 1 << bit
        if bit == ctx_bits - 1:
            mask |= mask >> 1
        got = [swap(s, "ctx", mask) for s in sums]
        if bit < ctx_bits - 1:
            for g, value in enumerate(got):
                sums[g] = add_part(sums[g], value)
            far += got

    weight_c = swap(output_weight, "head", 1)

    queries, near, states = [], [], []
    for c in range(spans):
        group = c * GROUPS // spans
        vals, pair = near_sums[group]
        q, part, state = span_part(
            c, spans, far_x[group], w_far, p_far, vals, pair, mixing, states, pieces, far
        )
        queries.append(q)
        near.append(part)
        states.append(state)

    gain = out_gain.reshape(1, width)
    step = SPAN // FIRST
    chunks = [(0, k * step, step) for k in range(FIRST)]
    chunks += [(c, 0, SPAN) for c in range(1, spans)]
    hidden, hidden_c = [], []
    for chunk in chunks:
        hid = hidden_part(
            chunk, queries[chunk[0]], got, pieces, mixing, near[chunk[0]], gain, levels - 1
        )
        hidden.append(hid)
        hidden_c.append(swap(hid, "head", 1))
    arrived = []
    for mask, w_own in zip(masks, w_outs):
        (w_other,) = fetch((weight_c, 1, block, (mask,)))
        for k in range(len(chunks)):
            part = out_part(hidden[k], hidden_c[k], w_own, w_other)
            arrived.append(swap(part, "head", mask))
    w_own, w_other = fetch((from_hbm(output_weight), 1, block, (0,)), (weight_c, 1, block, (0,)))
    own = own_part(hidden, hidden_c, w_own, w_other)
    n = len(chunks)
    early = [a for k, a in enumerate(arrived) if k % n < n - 1]
    out = sum_part(own, early, n - 1)
    return last_part(own, out, arrived[n - 1 :: n])


def solution(mesh):
    return jax.shard_map(
        local,
        mesh=mesh,
        in_specs=(
            P("ctx", "head"),
            P(),
            P(None, "head"),
            P("head", None),
            P("ctx", None),
            P(None, None, "head"),
            P("head"),
        ),
        out_specs=P("ctx", "head"),
        check_vma=False,
    )
```
